32 devices in a mesh: groups: 1, tile: 32 (over z, y, x, core).
Axes of the slice: x: 2, y: 2, z: 4, core: 2. Of those that a mesh axis runs over, the one named last changes fastest.
Arguments:
- tiles: bfloat16 [256, 64, 2048], P(('groups', 'tile')), may hold values from -6 to 6
- slide_of: int32 [256], P(('groups', 'tile')), may hold values from 0 to 3, as said below
- valid_count: int32 [32], P(('groups', 'tile')), may hold values from 1 to 8, as said below
- labels: int32 [4], P('groups'), may hold values from 0 to 1
- w_reduce: bfloat16 [2048, 1024], replicated, may hold values from -0.125 to 0.125
- w_expand: bfloat16 [1024, 2048], replicated, may hold values from -0.1875 to 0.1875
- queries: bfloat16 [64, 2048], replicated, may hold values from -16 to 16
- cls_weight: bfloat16 [64, 2048], replicated, may hold values from -0.0625 to 0.0625
Outputs:
- slide_loss: float32 [4], P('groups')
- d_queries: float32 [64, 2048], P('groups')
- d_reduce: float32 [2048, 1024], P(('groups', 'tile'))
- d_expand_t: float32 [2048, 1024], P(('groups', 'tile'))
The draws below stay inside these ranges and needn't reach their ends.
Inputs may be any that keep to these rules, and one draw needn't show every extreme that they name: `slide_of`: every slide has a valid tile. `valid_count`: some device has all 8 slots valid.
All inputs are finite; a program needn't handle non-finite values.
Results may differ from the reference program's by a relative error of at most 0.0039.
Values sent between devices are 32-bit elements; how exact they have to be, the bound alone decides.
A program may use at most 192 MiB of HBM per device.

```python
import jax
import jax.numpy as jnp
from jax import lax

D = 2048
MID = 1024
POS = 64
QUERIES = 64
TILE_DEV = 8
SLIDES = 4
TILES = 256


def draw_slide_of(key, part):
    places = jnp.arange(TILES).astype(jnp.int32)
    picked = jax.random.randint(key, (TILES,), 0, SLIDES).astype(jnp.int32)
    first = places // TILE_DEV % SLIDES
    return jnp.where(places % TILE_DEV == 0, first, picked).astype(jnp.int32)


def draw_valid_count(key, part):
    devices_here = TILES // TILE_DEV
    first_key = jax.random.fold_in(key, 11)
    second_key = jax.random.fold_in(key, 23)
    counts = jax.random.randint(first_key, (devices_here,), 1, TILE_DEV + 1).astype(jnp.int32)
    chosen = jax.random.randint(second_key, (), 0, devices_here).astype(jnp.int32)
    return jnp.where(jnp.arange(devices_here).astype(jnp.int32) == chosen, TILE_DEV, counts).astype(jnp.int32)


def draw_queries(key, part):
    base = jax.random.normal(key, (QUERIES, D), jnp.float32)
    return jnp.clip(base, -6.0, 6.0).astype(jnp.bfloat16)


def with_ends(values, own_key, smallest, top_value):
    spot = [jax.random.randint(jax.random.fold_in(own_key, axis), (), 0, length) for axis, length in enumerate(values.shape)]
    widest = values.shape.index(max(values.shape))
    neighbour = spot[:widest] + [(spot[widest] + 1) % values.shape[widest]] + spot[widest + 1:]
    return values.at[tuple(spot)].set(smallest).at[tuple(neighbour)].set(top_value)


def with_spikes(drawn, own_key, source, target, blocks, factor):
    owner, partner = [(jnp.arange(drawn.shape[axis_at]) // (drawn.shape[axis_at] // blocks)).reshape([-1 if axis == axis_at else 1 for axis in range(drawn.ndim)]) for axis_at in (source, target)]
    chosen = jax.random.permutation(own_key, blocks)[partner]
    strong = (owner == chosen) | (owner == (partner + blocks // 2) % blocks)
    return jnp.where(strong, factor * drawn, drawn)


def steps_of(rng, dims, shards, low, top_value):
    loudness = 1.0
    for dim, blocks in shards:
        steps = jax.random.uniform(jax.random.fold_in(jax.random.fold_in(rng, 6), dim), (blocks,), jnp.float32, low / len(shards), top_value / len(shards))
        loudness = loudness * jnp.repeat(jnp.exp(steps), dims[dim] // blocks).reshape((-1,) + (1,) * (len(dims) - 1 - dim))
    return loudness


def noise(rng, extent, width, bound, cuts=(), held_as=jnp.bfloat16):
    result = width * jax.random.normal(rng, extent, jnp.float32)
    if cuts:
        result = result * steps_of(rng, extent, cuts, -0.22, 0.18)
    return jnp.clip(result, -bound, bound).astype(held_as)


def noise_with(rng, extent, spread, bound, split, heavy, held_as=jnp.bfloat16):
    entries = spread * jax.random.normal(rng, extent, jnp.float32)
    if split:
        entries = entries * steps_of(rng, extent, split, -0.22, 0.18)
    return jnp.clip(with_spikes(entries, jax.random.fold_in(rng, 3), *heavy), -bound, bound).astype(held_as)


def setup_inputs(seed: int = 0, part: int = 0) -> dict:
    arg_keys = jax.random.split(jax.random.key(seed), 9)
    part_splits = jax.random.split(jax.random.fold_in(arg_keys[8], part), 9)
    return {
        "tiles": noise_with(part_splits[0], (TILES, POS, D), 1.0, 6.0, ((0, 32),), (0, 2, 32, 2.75)),
        "slide_of": draw_slide_of(jax.random.fold_in(jax.random.fold_in(arg_keys[8], part), 71), part),
        "valid_count": draw_valid_count(jax.random.fold_in(jax.random.fold_in(arg_keys[8], part), 71), part),
        "labels": with_ends(jax.random.randint(part_splits[3], (SLIDES,), 0, 2), jax.random.fold_in(part_splits[3], 1), 0, 1).astype(jnp.int32),
        "w_reduce": noise(arg_keys[4], (D, MID), D ** -0.5, 0.125),
        "w_expand": noise(arg_keys[5], (MID, D), MID ** -0.5, 0.1875),
        "queries": draw_queries(jax.random.fold_in(arg_keys[8], 71), part),
        "cls_weight": noise(arg_keys[7], (QUERIES, D), (QUERIES * D // 16) ** -0.5, 0.0625),
    }


HIGH = lax.Precision.HIGHEST

def slope(values):
    sig = jax.nn.sigmoid(values)
    return sig * (1.0 + values * (1.0 - sig))

def encode(block, w_reduce, w_expand):
    tile_rows = block.reshape(-1, D)
    pre_mid = jnp.dot(tile_rows, w_reduce, preferred_element_type=jnp.float32)
    hidden_act = jax.nn.silu(pre_mid).astype(jnp.bfloat16)
    pre_out = tile_rows.astype(jnp.float32) + jnp.dot(hidden_act, w_expand, preferred_element_type=jnp.float32)
    return (tile_rows, pre_mid, hidden_act, pre_out)

def reference(tiles, slide_of, valid_count, labels, w_reduce, w_expand, queries, cls_weight):
    blocks = tiles.reshape(-1, TILE_DEV, POS, D)

    def embed_block(block):
        pre_out = encode(block, w_reduce, w_expand)[3]
        return jax.nn.silu(pre_out).reshape(TILE_DEV, POS, D).mean(axis=1)
    embed = lax.map(embed_block, blocks).reshape(-1, D)
    places = jnp.arange(TILES).astype(jnp.int32)
    valid = places % TILE_DEV < valid_count[places // TILE_DEV]
    member = ((slide_of[:, None] == jnp.arange(SLIDES).astype(jnp.int32)[None, :]) & valid[:, None]).astype(jnp.float32)
    query_vals = queries.astype(jnp.float32)
    inv_root = 1.0 / jnp.sqrt(jnp.float32(D))
    scores = jnp.dot(embed, query_vals.T, precision=HIGH) * inv_root
    top_scores = lax.optimization_barrier(jnp.max(jnp.where(member[:, :, None] > 0, scores[:, None, :], -1e+30), axis=0))
    tile_top = jnp.dot(member, top_scores, precision=HIGH)
    weights = jnp.where(valid[:, None], jnp.exp(jnp.where(valid[:, None], scores - tile_top, 0.0)), 0.0)
    totals = jnp.dot(member.T, weights, precision=HIGH)
    numerators = jnp.einsum('ts,tq,td->sqd', member, weights, embed, precision=HIGH)
    pooled = numerators / totals[:, :, None]
    class_vals = cls_weight.astype(jnp.float32)
    logit = lax.optimization_barrier(jnp.sum(pooled * class_vals[None], axis=(1, 2)))
    targets = labels.astype(jnp.float32)
    slide_loss = jax.nn.softplus(logit) - targets * logit
    dlogit = (jax.nn.sigmoid(logit) - targets) / SLIDES
    dpooled = dlogit[:, None, None] * class_vals[None]
    tile_totals = jnp.where(valid[:, None], jnp.dot(member, totals, precision=HIGH), 1.0)
    prob = weights / tile_totals
    grad_dot = jnp.einsum('ts,sqd,td->tq', member, dpooled, embed, precision=HIGH)
    pooled_dot = lax.optimization_barrier(jnp.sum(dpooled * pooled, axis=2))
    dscore = prob * (grad_dot - jnp.dot(member, pooled_dot, precision=HIGH))
    dembed = jnp.dot(dscore, query_vals, precision=HIGH) * inv_root + jnp.einsum('ts,tq,sqd->td', member, prob, dpooled, precision=HIGH)
    d_queries = jnp.dot(dscore.T, embed, precision=HIGH) * inv_root
    dembed_blocks = dembed.reshape(-1, TILE_DEV, D)

    def advance(acc_pair, pieces):
        block, block_grad = pieces
        tile_rows, pre_mid, hidden_act, pre_out = encode(block, w_reduce, w_expand)
        dout = slope(pre_out).reshape(TILE_DEV, POS, D) * (block_grad[:, None, :] / POS)
        dout = dout.reshape(-1, D).astype(jnp.bfloat16)
        dmid = jnp.dot(dout, w_expand.T, preferred_element_type=jnp.float32)
        dpre_mid = (dmid * slope(pre_mid)).astype(jnp.bfloat16)
        grad_red = acc_pair[0] + jnp.dot(tile_rows.T, dpre_mid, preferred_element_type=jnp.float32)
        grad_exp = acc_pair[1] + jnp.dot(dout.T, hidden_act, preferred_element_type=jnp.float32)
        return ((grad_red, grad_exp), None)
    zeros_pair = (jnp.zeros((D, MID), jnp.float32), jnp.zeros((D, MID), jnp.float32))
    grads_pair, _ = lax.scan(advance, zeros_pair, (blocks, dembed_blocks))
    return (slide_loss, d_queries, grads_pair[0], grads_pair[1])
```

```python
import functools

import jax
import jax.numpy as jnp
import numpy as np
from jax import lax
from jax.experimental import pallas as pl
from jax.experimental.pallas import tpu as pltpu
from jax.sharding import PartitionSpec as P

CHUNK = 128
WIDE = 256
LAG = 5
KINDS = (0, 1, 2, 0, 1, 2, 0, 1)
MESH = pl.DeviceIdType.MESH


def bit_orders(count):
    bits = count.bit_length() - 1
    ring = list(range(1, bits))
    if bits != 5:
        return [[0] + ring[r:] + ring[:r] for r in (0, 1, 2)]
    return [[0, 1, 2, 3, 4], [0, 2, 1, 3, 4], [0, 3, 4, 1, 2]]


def place_of(block, order):
    place = 0
    for bit in order:
        place = place * 2 + (block // (1 << bit)) % 2
    return place


def three_pieces(values):
    high = values.astype(jnp.bfloat16).astype(jnp.float32)
    rest = values - high
    middle = rest.astype(jnp.bfloat16).astype(jnp.float32)
    return high, middle, rest - middle


def step_kernel(count, slides, positions, orders, slide_ref, valid_ref, label_ref, tiles_ref, reduce_ref, expand_ref,
                query_ref, class_ref, red_ref, exp_ref, query_out_ref, loss_ref, *scratch):
    width, middle = reduce_ref.shape
    rows_here = tiles_ref.shape[0]
    here_tiles = rows_here // positions
    queries = query_ref.shape[0]
    lanes = 2 * queries
    per_matrix = middle // CHUNK
    chunks = 2 * per_matrix
    grads = scratch[:chunks]
    lands = scratch[chunks:2 * chunks]
    (x, wr, we, both, hidden, slope_mid, slope_out, dout, dpre, embed, part, parts_all,
     query_sum, query_land, query_full, load_sem, part_send, part_recv, send_sem, recv_sem, query_send, query_recv,
     ) = scratch[2 * chunks:]
    steps = len(orders[0])
    me = lax.axis_index("tile")
    rows = width // count
    query_rows = query_sum.shape[0] // count
    inv_root = np.float32(1.0) / np.sqrt(np.float32(width))
    f32 = jnp.float32

    barrier = pltpu.get_barrier_semaphore()

    @pl.loop(1, count)
    def _(hop):
        pl.semaphore_signal(barrier, inc=1, device_id={"tile": lax.rem(me + hop, count)}, device_id_type=MESH)

    mid_blocks = middle // WIDE
    out_blocks = width // WIDE
    def load(source, target, at):
        copy = pltpu.make_async_copy(source, target, load_sem.at[at])
        copy.start()
        return copy
    def columns(ref, at):
        return ref.at[:, pl.ds(at * WIDE, WIDE)]
    x_load = load(tiles_ref, x, 0)
    wr_loads = [load(columns(reduce_ref, at), columns(wr, at), 4 + at) for at in range(mid_blocks)]
    we_load = load(expand_ref, we, 1)
    both_loads = [load(query_ref, both.at[pl.ds(0, queries)], 2), load(class_ref, both.at[pl.ds(queries, queries)], 3)]

    x_load.wait()
    for at in range(mid_blocks):
        wr_loads[at].wait()
        cols = slice(at * WIDE, (at + 1) * WIDE)
        pre = jnp.dot(x[...], wr[:, cols], preferred_element_type=f32)
        sig = 0.5 * jnp.tanh(0.5 * pre) + 0.5
        act = pre * sig
        hidden[:, cols] = act.astype(jnp.bfloat16)
        slope_mid[:, cols] = sig + act * (1.0 - sig)
    we_load.wait()

    @pl.loop(0, out_blocks)
    def _(at):
        cols = pl.ds(pl.multiple_of(at * WIDE, WIDE), WIDE)
        pre = x[:, cols].astype(f32) + jnp.dot(hidden[...], we[:, cols], preferred_element_type=f32)
        sig = 0.5 * jnp.tanh(0.5 * pre) + 0.5
        act = pre * sig
        slope_out[:, cols] = sig + act * (1.0 - sig)
        embed[:, cols] = jnp.sum(act.reshape(here_tiles, positions, WIDE), axis=1) * (1.0 / positions)

    for copy in both_loads:
        copy.wait()

    embeds = embed[...]
    pieces = three_pieces(embeds)
    score3 = lax.dot_general(jnp.concatenate(pieces, axis=0).astype(jnp.bfloat16), both[...],
                             (((1,), (1,)), ((), ())), preferred_element_type=f32)
    both_dot = score3[:here_tiles] + score3[here_tiles:2 * here_tiles] + score3[2 * here_tiles:]
    sub = lax.broadcasted_iota(jnp.int32, (here_tiles, lanes), 0)
    lane = lax.broadcasted_iota(jnp.int32, (here_tiles, lanes), 1)
    first = lane < queries
    scores = both_dot * inv_root
    class_dot = pltpu.roll(both_dot, queries, axis=1)
    slide_vec = jnp.zeros((here_tiles, lanes), jnp.int32)
    for tile in range(here_tiles):
        slide_vec = jnp.where(sub == tile, slide_ref[tile], slide_vec)
    valid = sub < valid_ref[0]
    members = [(slide_vec == slide) & valid for slide in range(slides)]
    for slide in range(slides):
        top = jnp.max(jnp.where(members[slide], scores, -1e30), axis=0, keepdims=True)
        weight = jnp.where(members[slide], jnp.exp(jnp.where(members[slide], scores - top, 0.0)), 0.0)
        total = jnp.sum(weight, axis=0, keepdims=True)
        dots = jnp.sum(weight * class_dot, axis=0, keepdims=True)
        part[slide:slide + 1, :] = jnp.where(first[:1], top, pltpu.roll(total, queries, axis=1))
        part[slides + slide:slides + slide + 1, :] = jnp.where(first[:1], dots, 0.0)

    pl.semaphore_wait(barrier, count - 1)

    def part_copy(hop, slot):
        return pltpu.make_async_remote_copy(
            src_ref=part, dst_ref=parts_all.at[slot], send_sem=part_send.at[hop], recv_sem=part_recv.at[hop],
            device_id={"tile": lax.rem(me + hop, count)}, device_id_type=MESH)

    @pl.loop(1, count)
    def _(hop):
        part_copy(hop, me).start()

    parts_all[me] = part[...]

    @pl.loop(1, count)
    def _(hop):
        part_copy(hop, lax.rem(me - hop + count, count)).wait_recv()

    gathered = parts_all[...]
    tops = jnp.max(gathered, axis=0)
    rescale = jnp.exp(gathered - tops[None])
    totals = jnp.sum(rescale * pltpu.roll(gathered, queries, axis=2), axis=0)
    ratio = jnp.sum(rescale * pltpu.roll(gathered, slides, axis=1), axis=0) / totals
    used = first & (sub < slides)
    logit = jnp.sum(jnp.where(used, ratio, 0.0), axis=1, keepdims=True) + jnp.zeros((here_tiles, lanes), f32)
    target_vec = jnp.zeros((here_tiles, lanes), jnp.int32)
    for slide in range(slides):
        target_vec = jnp.where(sub == slide, label_ref[slide], target_vec)
    targets = target_vec.astype(f32)
    loss_ref[...] = jnp.maximum(logit, 0.0) + jnp.log1p(jnp.exp(-jnp.abs(logit))) - targets * logit
    dlogit = (jax.nn.sigmoid(logit) - targets) * (1.0 / slides)

    def per_tile(values):
        result = jnp.zeros((here_tiles, lanes), f32)
        for slide in range(slides):
            result = jnp.where(members[slide], values[slide:slide + 1, :], result)
        return result

    live = valid & first
    weights = jnp.where(live, jnp.exp(jnp.where(live, scores - per_tile(tops), 0.0)), 0.0)
    prob_grad = jnp.where(live, weights / jnp.where(live, per_tile(totals), 1.0) * per_tile(dlogit), 0.0)
    dscore = jnp.where(live, prob_grad * (class_dot - per_tile(ratio)), 0.0) * inv_root
    coef = dscore + pltpu.roll(prob_grad, queries, axis=1)
    dembed3 = jnp.dot(jnp.concatenate(three_pieces(coef), axis=0).astype(jnp.bfloat16), both[...],
                      preferred_element_type=f32)
    embed[...] = (dembed3[:here_tiles] + dembed3[here_tiles:2 * here_tiles] + dembed3[2 * here_tiles:]) * (1.0 / positions)

    for tile in range(here_tiles):
        span_rows = slice(tile * positions, (tile + 1) * positions)
        dout[span_rows, :] = (slope_out[span_rows, :] * embed[tile:tile + 1, :]).astype(jnp.bfloat16)

    partners = [me + (1 << bit) * (1 - 2 * ((me // (1 << bit)) % 2)) for bit in range(steps)]

    def span(order, step, unit):
        half = count >> (step + 1)
        base = 0
        for at in range(step):
            base = base + ((me // (1 << order[at])) % 2) * (count >> (at + 1))
        mine = (me // (1 << order[step])) % 2
        keep = pl.multiple_of((base + mine * half) * unit, unit)
        give = pl.multiple_of((base + (1 - mine) * half) * unit, unit)
        return keep, give, half * unit

    def land_at(step, unit):
        return (count - (count >> step)) * unit

    def begin(source, land, order, step, unit, sends, recvs):
        keep, give, size = span(order, step, unit)
        copy = pltpu.make_async_remote_copy(
            src_ref=source.at[pl.ds(give, size)],
            dst_ref=land.at[pl.ds(land_at(step, unit), size)],
            send_sem=sends, recv_sem=recvs,
            device_id={"tile": partners[order[step]]},
            device_id_type=MESH,
        )
        copy.start()
        return copy

    def add(source, land, order, step, unit):
        keep, give, size = span(order, step, unit)
        piece = min(size, 256)

        @pl.loop(0, size // piece)
        def _(at):
            here = pl.ds(pl.multiple_of(keep + at * piece, piece), piece)
            there = pl.ds(pl.multiple_of(land_at(step, unit) + at * piece, piece), piece)
            source[here, :] = source[here, :] + land[there, :]

    def order_of(chunk):
        return orders[KINDS[chunk % len(KINDS)]]

    copies = {}

    def send(step, chunk):
        copies[step, chunk] = begin(grads[chunk], lands[chunk], order_of(chunk), step, rows,
                                    send_sem.at[step, chunk], recv_sem.at[step, chunk])

    query_order = orders[0]
    query_copies = []

    def query_start():
        terms = three_pieces(dscore)
        sides = three_pieces(embeds)
        left = jnp.concatenate([terms[0], terms[0], terms[1], terms[1], terms[0], terms[2]], axis=0)
        right = jnp.concatenate([sides[0], sides[1], sides[0], sides[1], sides[2], sides[0]], axis=0)
        product = lax.dot_general(left.astype(jnp.bfloat16), right.astype(jnp.bfloat16), (((0,), (0,)), ((), ())),
                                  preferred_element_type=f32)
        for above in range(queries // 8):
            for beside in range(width // 128):
                at = (above * (width // 128) + beside) * 8
                query_sum[at:at + 8, :] = product[above * 8:above * 8 + 8, beside * 128:beside * 128 + 128]
        query_copies.append(begin(query_sum, query_land, query_order, 0, query_rows,
                                  query_send.at[0], query_recv.at[0]))

    def share(step):
        keep, give, size = span(query_order, step, query_rows)
        held = query_full.at[pl.ds(keep, size)]
        copy = pltpu.make_async_remote_copy(
            src_ref=held, dst_ref=held,
            send_sem=query_send.at[steps + step], recv_sem=query_recv.at[steps + step],
            device_id={"tile": partners[query_order[step]]},
            device_id_type=MESH,
        )
        copy.start()
        return copy

    def advance_query():
        done = len(query_copies) - 1
        query_copies[done].wait()
        if done < steps:
            add(query_sum, query_land, query_order, done, query_rows)
        if done < steps - 1:
            query_copies.append(begin(query_sum, query_land, query_order, done + 1, query_rows,
                                      query_send.at[done + 1], query_recv.at[done + 1]))
            return
        if done == steps - 1:
            own = pl.ds(pl.multiple_of(place_of(me, query_order) * query_rows, query_rows), query_rows)
            query_full[own, :] = query_sum[own, :]
        query_copies.append(share(2 * steps - 2 - done) if done < 2 * steps - 1 else None)

    per_wide = WIDE // rows

    def multiply(left, right, right_cols, chunk):
        @pl.loop(0, width // WIDE)
        def _(at):
            product = lax.dot_general(
                left[:, pl.ds(pl.multiple_of(at * WIDE, WIDE), WIDE)], right[:, right_cols],
                (((0,), (0,)), ((), ())), preferred_element_type=f32)
            for inner in range(per_wide):
                for side in range(WIDE // CHUNK):
                    place = place_of(at * per_wide + inner, order_of(chunk + side))
                    there = pl.ds(pl.multiple_of(place * rows, rows), rows)
                    grads[chunk + side][there, :] = product[
                        inner * rows:(inner + 1) * rows, side * CHUNK:(side + 1) * CHUNK]

    def produce(chunk):
        cols = slice(chunk % per_matrix * CHUNK, chunk % per_matrix * CHUNK + WIDE)
        if chunk < per_matrix:
            multiply(dout, hidden, cols, chunk)
        else:
            dmid = lax.dot_general(dout[...], we[cols, :], (((1,), (1,)), ((), ())), preferred_element_type=f32)
            dpre[...] = (dmid * slope_mid[:, cols]).astype(jnp.bfloat16)
            multiply(x, dpre, slice(0, WIDE), chunk)
        for side in range(WIDE // CHUNK):
            send(0, chunk + side)

    visits = sorted(
        [(step, chunk) for step in range(steps + 1) for chunk in range(chunks) if step or chunk % (WIDE // CHUNK) == 0],
        key=lambda visit: (visit[1] + LAG * visit[0], visit[1]),
    )
    made = 0
    every = 8
    for at, (step, chunk) in enumerate(visits):
        if step == 0:
            produce(chunk)
            if chunk == 0:
                query_start()
            continue
        made += 1
        if made % every == 0 and len(query_copies) <= 2 * steps:
            advance_query()
        order = order_of(chunk)
        copies[step - 1, chunk].wait()
        add(grads[chunk], lands[chunk], order, step - 1, rows)
        if step < steps:
            send(step, chunk)
        else:
            out_ref = (exp_ref, red_ref)[chunk // per_matrix]
            start = chunk % per_matrix * CHUNK
            out_ref[:, start:start + CHUNK] = grads[chunk][
                pl.ds(pl.multiple_of(place_of(me, order) * rows, rows), rows), :
            ]
    while len(query_copies) <= 2 * steps:
        advance_query()
    for above in range(queries // 8):
        for beside in range(width // 128):
            at = (above * (width // 128) + beside) * 8
            query_out_ref[above * 8:above * 8 + 8, beside * 128:beside * 128 + 128] = query_full[at:at + 8, :]

    @pl.loop(1, count)
    def _(hop):
        part_copy(hop, me).wait_send()


def hand_over_kernel(red_in, exp_in, query_in, loss_in, loss_out, query_out, red_out, exp_out, *scratch):
    buffers, (in_sems, out_sems) = scratch[:3], scratch[3:]
    pairs = ((query_in, query_out), (red_in, red_out), (exp_in, exp_out))
    loads = [pltpu.make_async_copy(pair[0], buffers[at], in_sems.at[at]) for at, pair in enumerate(pairs)]
    stores = [pltpu.make_async_copy(buffers[at], pair[1], out_sems.at[at]) for at, pair in enumerate(pairs)]
    for load in loads:
        load.start()
    for slide in range(loss_out.shape[0]):
        loss_out[slide] = loss_in[slide, 0]
    for load, store in zip(loads, stores):
        load.wait()
        store.start()
    for store in stores:
        store.wait()


def on_device(count, tiles, slide_of, valid_count, labels, w_reduce, w_expand, queries, cls_weight):
    here_tiles, positions, width = tiles.shape
    slides = labels.shape[0]
    middle = w_reduce.shape[1]
    count_queries = queries.shape[0]
    rows_here = here_tiles * positions
    orders = bit_orders(count)
    steps = len(orders[0])
    chunks = 2 * middle // CHUNK
    lanes = 2 * count_queries
    vmem = pl.BlockSpec(memory_space=pltpu.VMEM)
    smem = pl.BlockSpec(memory_space=pltpu.SMEM)
    anywhere = pl.BlockSpec(memory_space=pl.ANY)
    f32, bf16 = jnp.float32, jnp.bfloat16
    flat = (count_queries * width // 128, 128)
    red, exp, shared, loss = pl.pallas_call(
        functools.partial(step_kernel, count, slides, positions, orders),
        out_shape=(
            jax.ShapeDtypeStruct((width // count, middle), f32),
            jax.ShapeDtypeStruct((width // count, middle), f32),
            jax.ShapeDtypeStruct((count_queries, width), f32),
            jax.ShapeDtypeStruct((here_tiles, lanes), f32),
        ),
        in_specs=[smem] * 3 + [anywhere] * 5,
        out_specs=(vmem,) * 4,
        scratch_shapes=(
            [pltpu.VMEM((width, CHUNK), f32)] * (2 * chunks)
            + [
                pltpu.VMEM((rows_here, width), bf16),
                pltpu.VMEM((width, middle), bf16),
                pltpu.VMEM((middle, width), bf16),
                pltpu.VMEM((lanes, width), bf16),
                pltpu.VMEM((rows_here, middle), bf16),
                pltpu.VMEM((rows_here, middle), f32),
                pltpu.VMEM((rows_here, width), f32),
                pltpu.VMEM((rows_here, width), bf16),
                pltpu.VMEM((rows_here, WIDE), bf16),
                pltpu.VMEM((here_tiles, width), f32),
                pltpu.VMEM((here_tiles, lanes), f32),
                pltpu.VMEM((count, here_tiles, lanes), f32),
                pltpu.VMEM(flat, f32),
                pltpu.VMEM(flat, f32),
                pltpu.VMEM(flat, f32),
                pltpu.SemaphoreType.DMA((4 + middle // WIDE,)),
                pltpu.SemaphoreType.DMA((count,)),
                pltpu.SemaphoreType.DMA((count,)),
                pltpu.SemaphoreType.DMA((steps, chunks)),
                pltpu.SemaphoreType.DMA((steps, chunks)),
                pltpu.SemaphoreType.DMA((2 * steps,)),
                pltpu.SemaphoreType.DMA((2 * steps,)),
            ]
        ),
        compiler_params=pltpu.CompilerParams(
            collective_id=0, has_side_effects=True, vmem_limit_bytes=62 * 1024 * 1024
        ),
    )(slide_of, valid_count, labels, tiles.reshape(rows_here, width), w_reduce, w_expand, queries, cls_weight)
    return pl.pallas_call(
        hand_over_kernel,
        out_shape=(
            jax.ShapeDtypeStruct((slides,), f32),
            jax.ShapeDtypeStruct(shared.shape, f32),
            jax.ShapeDtypeStruct(red.shape, f32),
            jax.ShapeDtypeStruct(exp.shape, f32),
        ),
        in_specs=[anywhere] * 3 + [vmem],
        out_specs=(smem,) + (anywhere,) * 3,
        scratch_shapes=[pltpu.VMEM(value.shape, f32) for value in (shared, red, exp)]
        + [pltpu.SemaphoreType.DMA((3,)), pltpu.SemaphoreType.DMA((3,))],
    )(red, exp, shared, loss)


def solution(mesh):
    return jax.shard_map(
        functools.partial(on_device, mesh.shape["tile"]),
        mesh=mesh,
        in_specs=(
            P(("groups", "tile"), None, None),
            P(("groups", "tile")),
            P(("groups", "tile")),
            P("groups"),
            P(),
            P(),
            P(),
            P(),
        ),
        out_specs=(
            P("groups"),
            P("groups", None),
            P(("groups", "tile"), None),
            P(("groups", "tile"), None),
        ),
        check_vma=False,
    )
```

```python
import functools

import jax
import jax.numpy as jnp
import numpy as np
from jax import lax
from jax.experimental import pallas as pl
from jax.experimental.pallas import tpu as pltpu
from jax.sharding import PartitionSpec as P

CHUNK = 128
WIDE = 256
TALL = 512
LAGS = tuple(4 * step for step in range(12))
KINDS = (0, 1, 2, 0, 1, 2, 0, 1)
MESH = pl.DeviceIdType.MESH


def bit_orders(count):
    bits = count.bit_length() - 1
    ring = list(range(1, bits))
    if bits != 5:
        return [[0] + ring[r:] + ring[:r] for r in (0, 1, 2)]
    return [[0, 1, 2, 3, 4], [0, 2, 1, 3, 4], [0, 3, 4, 1, 2]]


def place_of(block, order):
    place = 0
    for bit in order:
        place = place * 2 + (block // (1 << bit)) % 2
    return place


def three_pieces(values):
    high = values.astype(jnp.bfloat16).astype(jnp.float32)
    rest = values - high
    middle = rest.astype(jnp.bfloat16).astype(jnp.float32)
    return high, middle, rest - middle


def step_kernel(count, slides, positions, orders, slide_ref, valid_ref, label_ref, tiles_ref, reduce_ref, expand_ref,
                query_ref, class_ref, red_ref, exp_ref, query_out_ref, loss_ref, *scratch):
    width, middle = reduce_ref.shape
    rows_here = tiles_ref.shape[0]
    here_tiles = rows_here // positions
    queries = query_ref.shape[0]
    lanes = 2 * queries
    per_matrix = middle // CHUNK
    chunks = 2 * per_matrix
    grads = scratch[:chunks]
    lands = scratch[chunks:2 * chunks]
    (x, wr, we, both, hidden, slope_mid, slope_out, dout, x_turned, dout_turned, dpre, embed, part, parts_all,
     query_sum, query_land, query_full, load_sem, part_send, part_recv, send_sem, recv_sem, query_send, query_recv,
     ) = scratch[2 * chunks:]
    steps = len(orders[0])
    me = lax.axis_index("tile")
    rows = width // count
    query_rows = query_sum.shape[0] // count
    inv_root = np.float32(1.0) / np.sqrt(np.float32(width))
    f32 = jnp.float32

    barrier = pltpu.get_barrier_semaphore()

    @pl.loop(1, count)
    def _(hop):
        pl.semaphore_signal(barrier, inc=1, device_id={"tile": lax.rem(me + hop, count)}, device_id_type=MESH)

    mid_blocks = middle // WIDE
    out_blocks = width // WIDE
    def load(source, target, at):
        copy = pltpu.make_async_copy(source, target, load_sem.at[at])
        copy.start()
        return copy
    def columns(ref, at):
        return ref.at[:, pl.ds(at * WIDE, WIDE)]
    x_load = load(tiles_ref, x, 0)
    wr_loads = [load(columns(reduce_ref, at), columns(wr, at), 4 + at) for at in range(mid_blocks)]
    we_load = load(expand_ref, we, 1)
    both_loads = [load(query_ref, both.at[pl.ds(0, queries)], 2), load(class_ref, both.at[pl.ds(queries, queries)], 3)]

    x_load.wait()
    for at in range(mid_blocks):
        wr_loads[at].wait()
        cols = slice(at * WIDE, (at + 1) * WIDE)
        pre = jnp.dot(x[...], wr[:, cols], preferred_element_type=f32)
        sig = 0.5 * jnp.tanh(0.5 * pre) + 0.5
        act = pre * sig
        hidden[:, cols] = act.astype(jnp.bfloat16)
        slope_mid[:, cols] = sig + act * (1.0 - sig)
    we_load.wait()

    for at in range(out_blocks):
        cols = slice(at * WIDE, (at + 1) * WIDE)
        pre = x[:, cols].astype(f32) + jnp.dot(hidden[...], we[:, cols], preferred_element_type=f32)
        sig = 0.5 * jnp.tanh(0.5 * pre) + 0.5
        act = pre * sig
        slope_out[:, cols] = sig + act * (1.0 - sig)
        embed[:, cols] = jnp.sum(act.reshape(here_tiles, positions, WIDE), axis=1) * (1.0 / positions)

    for copy in both_loads:
        copy.wait()

    embeds = embed[...]
    pieces = three_pieces(embeds)
    score3 = lax.dot_general(jnp.concatenate(pieces, axis=0).astype(jnp.bfloat16), both[...],
                             (((1,), (1,)), ((), ())), preferred_element_type=f32)
    both_dot = score3[:here_tiles] + score3[here_tiles:2 * here_tiles] + score3[2 * here_tiles:]
    sub = lax.broadcasted_iota(jnp.int32, (here_tiles, lanes), 0)
    lane = lax.broadcasted_iota(jnp.int32, (here_tiles, lanes), 1)
    first = lane < queries
    scores = both_dot * inv_root
    class_dot = pltpu.roll(both_dot, queries, axis=1)
    slide_vec = jnp.zeros((here_tiles, lanes), jnp.int32)
    for tile in range(here_tiles):
        slide_vec = jnp.where(sub == tile, slide_ref[tile], slide_vec)
    valid = sub < valid_ref[0]
    members = [(slide_vec == slide) & valid for slide in range(slides)]
    for slide in range(slides):
        top = jnp.max(jnp.where(members[slide], scores, -1e30), axis=0, keepdims=True)
        weight = jnp.where(members[slide], jnp.exp(jnp.where(members[slide], scores - top, 0.0)), 0.0)
        total = jnp.sum(weight, axis=0, keepdims=True)
        dots = jnp.sum(weight * class_dot, axis=0, keepdims=True)
        part[slide:slide + 1, :] = jnp.where(first[:1], top, pltpu.roll(total, queries, axis=1))
        part[slides + slide:slides + slide + 1, :] = jnp.where(first[:1], dots, 0.0)

    pl.semaphore_wait(barrier, count - 1)

    def part_copy(hop, slot):
        return pltpu.make_async_remote_copy(
            src_ref=part, dst_ref=parts_all.at[slot], send_sem=part_send.at[hop], recv_sem=part_recv.at[hop],
            device_id={"tile": lax.rem(me + hop, count)}, device_id_type=MESH)

    @pl.loop(1, count)
    def _(hop):
        part_copy(hop, me).start()

    parts_all[me] = part[...]
    for at in range(out_blocks):
        cols = slice(at * WIDE, (at + 1) * WIDE)
        x_turned[cols, :] = x[:, cols].T

    @pl.loop(1, count)
    def _(hop):
        part_copy(hop, lax.rem(me - hop + count, count)).wait_recv()

    gathered = parts_all[...]
    tops = jnp.max(gathered, axis=0)
    rescale = jnp.exp(gathered - tops[None])
    totals = jnp.sum(rescale * pltpu.roll(gathered, queries, axis=2), axis=0)
    ratio = jnp.sum(rescale * pltpu.roll(gathered, slides, axis=1), axis=0) / totals
    used = first & (sub < slides)
    logit = jnp.sum(jnp.where(used, ratio, 0.0), axis=1, keepdims=True) + jnp.zeros((here_tiles, lanes), f32)
    target_vec = jnp.zeros((here_tiles, lanes), jnp.int32)
    for slide in range(slides):
        target_vec = jnp.where(sub == slide, label_ref[slide], target_vec)
    targets = target_vec.astype(f32)
    loss_ref[...] = jnp.maximum(logit, 0.0) + jnp.log1p(jnp.exp(-jnp.abs(logit))) - targets * logit
    dlogit = (jax.nn.sigmoid(logit) - targets) * (1.0 / slides)

    def per_tile(values):
        result = jnp.zeros((here_tiles, lanes), f32)
        for slide in range(slides):
            result = jnp.where(members[slide], values[slide:slide + 1, :], result)
        return result

    live = valid & first
    weights = jnp.where(live, jnp.exp(jnp.where(live, scores - per_tile(tops), 0.0)), 0.0)
    prob_grad = jnp.where(live, weights / jnp.where(live, per_tile(totals), 1.0) * per_tile(dlogit), 0.0)
    dscore = jnp.where(live, prob_grad * (class_dot - per_tile(ratio)), 0.0) * inv_root
    coef = dscore + pltpu.roll(prob_grad, queries, axis=1)
    dembed3 = jnp.dot(jnp.concatenate(three_pieces(coef), axis=0).astype(jnp.bfloat16), both[...],
                      preferred_element_type=f32)
    embed[...] = (dembed3[:here_tiles] + dembed3[here_tiles:2 * here_tiles] + dembed3[2 * here_tiles:]) * (1.0 / positions)

    for at in range(out_blocks):
        cols = slice(at * WIDE, (at + 1) * WIDE)
        block = jnp.concatenate(
            [slope_out[tile * positions:(tile + 1) * positions, cols] * embed[tile:tile + 1, cols]
             for tile in range(here_tiles)], axis=0).astype(jnp.bfloat16)
        dout[:, cols] = block
        dout_turned[cols, :] = block.T

    partners = [me + (1 << bit) * (1 - 2 * ((me // (1 << bit)) % 2)) for bit in range(steps)]

    def span(order, step, unit):
        half = count >> (step + 1)
        base = 0
        for at in range(step):
            base = base + ((me // (1 << order[at])) % 2) * (count >> (at + 1))
        mine = (me // (1 << order[step])) % 2
        keep = pl.multiple_of((base + mine * half) * unit, unit)
        give = pl.multiple_of((base + (1 - mine) * half) * unit, unit)
        return keep, give, half * unit

    def land_at(step, unit):
        return (count - (count >> step)) * unit

    def begin(source, land, order, step, unit, sends, recvs):
        keep, give, size = span(order, step, unit)
        copy = pltpu.make_async_remote_copy(
            src_ref=source.at[pl.ds(give, size)],
            dst_ref=land.at[pl.ds(land_at(step, unit), size)],
            send_sem=sends, recv_sem=recvs,
            device_id={"tile": partners[order[step]]},
            device_id_type=MESH,
        )
        copy.start()
        return copy

    def add(source, land, order, step, unit):
        keep, give, size = span(order, step, unit)
        piece = min(size, 256)

        @pl.loop(0, size // piece)
        def _(at):
            here = pl.ds(pl.multiple_of(keep + at * piece, piece), piece)
            there = pl.ds(pl.multiple_of(land_at(step, unit) + at * piece, piece), piece)
            source[here, :] = source[here, :] + land[there, :]

    def order_of(chunk):
        return orders[KINDS[chunk % len(KINDS)]]

    copies = {}

    def send(step, chunk):
        copies[step, chunk] = begin(grads[chunk], lands[chunk], order_of(chunk), step, rows,
                                    send_sem.at[step, chunk], recv_sem.at[step, chunk])

    query_order = orders[0]
    query_copies = []

    def query_start():
        terms = three_pieces(dscore)
        sides = three_pieces(embeds)
        left = jnp.concatenate([terms[0], terms[0], terms[1], terms[1], terms[0], terms[2]], axis=0)
        right = jnp.concatenate([sides[0], sides[1], sides[0], sides[1], sides[2], sides[0]], axis=0)
        product = lax.dot_general(left.astype(jnp.bfloat16), right.astype(jnp.bfloat16), (((0,), (0,)), ((), ())),
                                  preferred_element_type=f32)
        for above in range(queries // 8):
            for beside in range(width // 128):
                at = (above * (width // 128) + beside) * 8
                query_sum[at:at + 8, :] = product[above * 8:above * 8 + 8, beside * 128:beside * 128 + 128]
        query_copies.append(begin(query_sum, query_land, query_order, 0, query_rows,
                                  query_send.at[0], query_recv.at[0]))

    def share(step):
        keep, give, size = span(query_order, step, query_rows)
        held = query_full.at[pl.ds(keep, size)]
        copy = pltpu.make_async_remote_copy(
            src_ref=held, dst_ref=held,
            send_sem=query_send.at[steps + step], recv_sem=query_recv.at[steps + step],
            device_id={"tile": partners[query_order[step]]},
            device_id_type=MESH,
        )
        copy.start()
        return copy

    def advance_query():
        done = len(query_copies) - 1
        query_copies[done].wait()
        if done < steps:
            add(query_sum, query_land, query_order, done, query_rows)
        if done < steps - 1:
            query_copies.append(begin(query_sum, query_land, query_order, done + 1, query_rows,
                                      query_send.at[done + 1], query_recv.at[done + 1]))
            return
        if done == steps - 1:
            own = pl.ds(pl.multiple_of(place_of(me, query_order) * query_rows, query_rows), query_rows)
            query_full[own, :] = query_sum[own, :]
        query_copies.append(share(2 * steps - 2 - done) if done < 2 * steps - 1 else None)

    def multiply(left, right, right_cols, chunk):
        for at in range(width // TALL):
            product = jnp.dot(left[at * TALL:(at + 1) * TALL, :], right[:, right_cols], preferred_element_type=f32)
            for inner in range(TALL // rows):
                for side in range(WIDE // CHUNK):
                    place = place_of(at * (TALL // rows) + inner, order_of(chunk + side)) * rows
                    grads[chunk + side][place:place + rows, :] = product[
                        inner * rows:(inner + 1) * rows, side * CHUNK:(side + 1) * CHUNK]

    def produce(chunk):
        cols = slice(chunk % per_matrix * CHUNK, chunk % per_matrix * CHUNK + WIDE)
        if chunk < per_matrix:
            multiply(dout_turned, hidden, cols, chunk)
        else:
            dmid = lax.dot_general(dout[...], we[cols, :], (((1,), (1,)), ((), ())), preferred_element_type=f32)
            dpre[...] = (dmid * slope_mid[:, cols]).astype(jnp.bfloat16)
            multiply(x_turned, dpre, slice(0, WIDE), chunk)
        for side in range(WIDE // CHUNK):
            send(0, chunk + side)

    visits = sorted(
        [(step, chunk) for step in range(steps + 1) for chunk in range(chunks) if step or chunk % (WIDE // CHUNK) == 0],
        key=lambda visit: (visit[1] + LAGS[visit[0]], visit[1]),
    )
    made = 0
    every = 8
    for at, (step, chunk) in enumerate(visits):
        if step == 0:
            produce(chunk)
            if chunk == 0:
                query_start()
            continue
        made += 1
        if made % every == 0 and len(query_copies) <= 2 * steps:
            advance_query()
        order = order_of(chunk)
        copies[step - 1, chunk].wait()
        add(grads[chunk], lands[chunk], order, step - 1, rows)
        if step < steps:
            send(step, chunk)
        else:
            out_ref = (exp_ref, red_ref)[chunk // per_matrix]
            start = chunk % per_matrix * CHUNK
            out_ref[:, start:start + CHUNK] = grads[chunk][
                pl.ds(pl.multiple_of(place_of(me, order) * rows, rows), rows), :
            ]
    while len(query_copies) <= 2 * steps:
        advance_query()
    for above in range(queries // 8):
        for beside in range(width // 128):
            at = (above * (width // 128) + beside) * 8
            query_out_ref[above * 8:above * 8 + 8, beside * 128:beside * 128 + 128] = query_full[at:at + 8, :]

    @pl.loop(1, count)
    def _(hop):
        part_copy(hop, me).wait_send()


def hand_over_kernel(red_in, exp_in, query_in, loss_in, loss_out, query_out, red_out, exp_out, *scratch):
    buffers, (in_sems, out_sems) = scratch[:3], scratch[3:]
    pairs = ((query_in, query_out), (red_in, red_out), (exp_in, exp_out))
    loads = [pltpu.make_async_copy(pair[0], buffers[at], in_sems.at[at]) for at, pair in enumerate(pairs)]
    stores = [pltpu.make_async_copy(buffers[at], pair[1], out_sems.at[at]) for at, pair in enumerate(pairs)]
    for load in loads:
        load.start()
    for slide in range(loss_out.shape[0]):
        loss_out[slide] = loss_in[slide, 0]
    for load, store in zip(loads, stores):
        load.wait()
        store.start()
    for store in stores:
        store.wait()


def on_device(count, tiles, slide_of, valid_count, labels, w_reduce, w_expand, queries, cls_weight):
    here_tiles, positions, width = tiles.shape
    slides = labels.shape[0]
    middle = w_reduce.shape[1]
    count_queries = queries.shape[0]
    rows_here = here_tiles * positions
    orders = bit_orders(count)
    steps = len(orders[0])
    chunks = 2 * middle // CHUNK
    lanes = 2 * count_queries
    vmem = pl.BlockSpec(memory_space=pltpu.VMEM)
    smem = pl.BlockSpec(memory_space=pltpu.SMEM)
    anywhere = pl.BlockSpec(memory_space=pl.ANY)
    f32, bf16 = jnp.float32, jnp.bfloat16
    flat = (count_queries * width // 128, 128)
    red, exp, shared, loss = pl.pallas_call(
        functools.partial(step_kernel, count, slides, positions, orders),
        out_shape=(
            jax.ShapeDtypeStruct((width // count, middle), f32),
            jax.ShapeDtypeStruct((width // count, middle), f32),
            jax.ShapeDtypeStruct((count_queries, width), f32),
            jax.ShapeDtypeStruct((here_tiles, lanes), f32),
        ),
        in_specs=[smem] * 3 + [anywhere] * 5,
        out_specs=(vmem,) * 4,
        scratch_shapes=(
            [pltpu.VMEM((width, CHUNK), f32)] * (2 * chunks)
            + [
                pltpu.VMEM((rows_here, width), bf16),
                pltpu.VMEM((width, middle), bf16),
                pltpu.VMEM((middle, width), bf16),
                pltpu.VMEM((lanes, width), bf16),
                pltpu.VMEM((rows_here, middle), bf16),
                pltpu.VMEM((rows_here, middle), f32),
                pltpu.VMEM((rows_here, width), f32),
                pltpu.VMEM((rows_here, width), bf16),
                pltpu.VMEM((width, rows_here), bf16),
                pltpu.VMEM((width, rows_here), bf16),
                pltpu.VMEM((rows_here, WIDE), bf16),
                pltpu.VMEM((here_tiles, width), f32),
                pltpu.VMEM((here_tiles, lanes), f32),
                pltpu.VMEM((count, here_tiles, lanes), f32),
                pltpu.VMEM(flat, f32),
                pltpu.VMEM(flat, f32),
                pltpu.VMEM(flat, f32),
                pltpu.SemaphoreType.DMA((4 + middle // WIDE,)),
                pltpu.SemaphoreType.DMA((count,)),
                pltpu.SemaphoreType.DMA((count,)),
                pltpu.SemaphoreType.DMA((steps, chunks)),
                pltpu.SemaphoreType.DMA((steps, chunks)),
                pltpu.SemaphoreType.DMA((2 * steps,)),
                pltpu.SemaphoreType.DMA((2 * steps,)),
            ]
        ),
        compiler_params=pltpu.CompilerParams(
            collective_id=0, has_side_effects=True, vmem_limit_bytes=62 * 1024 * 1024
        ),
    )(slide_of, valid_count, labels, tiles.reshape(rows_here, width), w_reduce, w_expand, queries, cls_weight)
    return pl.pallas_call(
        hand_over_kernel,
        out_shape=(
            jax.ShapeDtypeStruct((slides,), f32),
            jax.ShapeDtypeStruct(shared.shape, f32),
            jax.ShapeDtypeStruct(red.shape, f32),
            jax.ShapeDtypeStruct(exp.shape, f32),
        ),
        in_specs=[anywhere] * 3 + [vmem],
        out_specs=(smem,) + (anywhere,) * 3,
        scratch_shapes=[pltpu.VMEM(value.shape, f32) for value in (shared, red, exp)]
        + [pltpu.SemaphoreType.DMA((3,)), pltpu.SemaphoreType.DMA((3,))],
    )(red, exp, shared, loss)


def solution(mesh):
    return jax.shard_map(
        functools.partial(on_device, mesh.shape["tile"]),
        mesh=mesh,
        in_specs=(
            P(("groups", "tile"), None, None),
            P(("groups", "tile")),
            P(("groups", "tile")),
            P("groups"),
            P(),
            P(),
            P(),
            P(),
        ),
        out_specs=(
            P("groups"),
            P("groups", None),
            P(("groups", "tile"), None),
            P(("groups", "tile"), None),
        ),
        check_vma=False,
    )
```

```python
import functools

import jax
import jax.numpy as jnp
import numpy as np
from jax import lax
from jax.experimental import pallas as pl
from jax.experimental.pallas import tpu as pltpu
from jax.sharding import PartitionSpec as P

CHUNK = 128
WIDE = 256
TALL = 512
LAG = 4
SPLIT = 1
KINDS = (
    2, 0, 1, 2, 0, 2, 0, 1, 0, 1, 1, 2, 0, 0, 1, 1,
)
STEPS = (
    -1, 257, -2, 1, -3, 17, 33, -4, -5, 81, 97, 113, 258, 65, -6, 129, 2, 34, 49, 161, 98, -7, 193, 114,
    259, 82, 66, 177, 145, -8, 50, 18, 130, 99, 162, 260, 67, 35, 178, 146, 194, 209, 51, 115, 241, 261, 19, 225,
    36, 163, 100, 262, 20, 242, 68, 116, 147, 131, 179, 52, 263, 195, 210, 164, 69, 101, 226, 243, 3, 83, 132, 148,
    196, 180, 227, 53, 21, 211, 37, 244, 4, 181, 264, 117, 133, 228, 84, 212, 265, 165, 245, 85, 5, 197, 229, 149,
    266, 213,
)
MESH = pl.DeviceIdType.MESH


def plan_of(count, blocks):
    bits = count.bit_length() - 1
    parts = blocks * (WIDE // CHUNK) * SPLIT
    if (bits, blocks) == (5, 8):
        orders = [[0, 1, 2, 3, 4], [0, 2, 1, 3, 4], [0, 3, 4, 1, 2]]
        return [orders[kind] for kind in KINDS], STEPS
    ring = list(range(1, bits))
    turns = [ring[turn:] + ring[:turn] for turn in (0, 1, 2)]
    orders = [[0] + turns[part // SPLIT % 8 % 3] for part in range(parts)]
    per_block = parts // blocks
    keyed = []
    for part in range(parts):
        if part % per_block == 0:
            keyed.append((part / SPLIT, -1 - part // per_block))
        for step in range(1, bits + 1):
            keyed.append((part / SPLIT + LAG * step, part * 16 + step))
    for step in range(1, 2 * bits + 1):
        keyed.append((step * 0.5 * LAG, parts * 16 + step))
    return orders, [code for key, code in sorted(keyed, key=lambda pair: pair[0])]


def place_of(block, order):
    place = 0
    for bit in order:
        place = place * 2 + (block // (1 << bit)) % 2
    return place


def three_pieces(values):
    high = values.astype(jnp.bfloat16).astype(jnp.float32)
    rest = values - high
    middle = rest.astype(jnp.bfloat16).astype(jnp.float32)
    return high, middle, rest - middle


def step_kernel(count, slides, positions, orders, order_of_steps, slide_any, valid_any, label_any, tiles_ref, reduce_ref, expand_ref,
                query_ref, class_ref, red_ref, exp_ref, query_out_ref, loss_ref, *scratch):
    width, middle = reduce_ref.shape
    rows_here = tiles_ref.shape[0]
    here_tiles = rows_here // positions
    queries = query_ref.shape[0]
    lanes = 2 * queries
    per_matrix = middle // CHUNK * SPLIT
    per_block = WIDE // CHUNK * SPLIT
    chunks = 2 * per_matrix
    grads = scratch[:chunks]
    lands = scratch[chunks:2 * chunks]
    (x, wr, we, both, hidden, slope_mid, slope_out, dout, x_turned, dout_turned, dpre, embed, part, parts_all, slide_ref, valid_ref, label_ref,
     query_sum, query_land, query_full, load_sem, part_send, part_recv, send_sem, recv_sem, query_send, query_recv,
     ) = scratch[2 * chunks:]
    steps = len(orders[0])
    me = lax.axis_index("tile")
    rows = width // count
    unit_rows = rows // SPLIT
    query_rows = query_sum.shape[0] // count
    inv_root = np.float32(1.0) / np.sqrt(np.float32(width))
    f32 = jnp.float32

    barrier = pltpu.get_barrier_semaphore()

    mid_blocks = middle // WIDE
    out_blocks = width // WIDE
    def load(source, target, at):
        copy = pltpu.make_async_copy(source, target, load_sem.at[at])
        copy.start()
        return copy
    def columns(ref, at):
        return ref.at[:, pl.ds(at * WIDE, WIDE)]
    x_load = load(tiles_ref, x, 0)
    for at in range(mid_blocks):
        load(columns(reduce_ref, at), columns(wr, at), 4 + at)
    we_load = load(expand_ref, we, 1)
    both_loads = [load(query_ref, both.at[pl.ds(0, queries)], 2), load(class_ref, both.at[pl.ds(queries, queries)], 3)]

    small_loads = [load(slide_any, slide_ref, 4 + mid_blocks), load(valid_any, valid_ref, 5 + mid_blocks),
                   load(label_any, label_ref, 6 + mid_blocks)]

    def wrapped(device):
        return jnp.where(device >= count, device - count, device)

    @pl.loop(1, count)
    def _(hop):
        pl.semaphore_signal(barrier, inc=1, device_id={"tile": wrapped(me + hop)}, device_id_type=MESH)

    x_load.wait()

    @pl.loop(0, mid_blocks)
    def _(at):
        cols = pl.ds(pl.multiple_of(at * WIDE, WIDE), WIDE)
        pltpu.make_async_copy(reduce_ref.at[:, cols], wr.at[:, cols], load_sem.at[4 + at]).wait()
        pre = jnp.dot(x[...], wr[:, cols], preferred_element_type=f32)
        sig = 0.5 * jnp.tanh(0.5 * pre) + 0.5
        act = pre * sig
        hidden[:, cols] = act.astype(jnp.bfloat16)
        slope_mid[:, cols] = sig + act * (1.0 - sig)
    we_load.wait()

    @pl.loop(0, width // TALL)
    def _(at):
        cols = pl.ds(pl.multiple_of(at * TALL, TALL), TALL)
        pre = x[:, cols].astype(f32) + jnp.dot(hidden[...], we[:, cols], preferred_element_type=f32)
        sig = 0.5 * jnp.tanh(0.5 * pre) + 0.5
        act = pre * sig
        slope_out[:, cols] = sig + act * (1.0 - sig)
        embed[:, cols] = jnp.sum(act.reshape(here_tiles, positions, TALL), axis=1) * (1.0 / positions)

    for copy in both_loads + small_loads:
        copy.wait()

    embeds = embed[...]
    pieces = three_pieces(embeds)
    score3 = lax.dot_general(jnp.concatenate(pieces, axis=0).astype(jnp.bfloat16), both[...],
                             (((1,), (1,)), ((), ())), preferred_element_type=f32)
    both_dot = score3[:here_tiles] + score3[here_tiles:2 * here_tiles] + score3[2 * here_tiles:]
    sub = lax.broadcasted_iota(jnp.int32, (here_tiles, lanes), 0)
    lane = lax.broadcasted_iota(jnp.int32, (here_tiles, lanes), 1)
    first = lane < queries
    scores = both_dot * inv_root
    class_dot = pltpu.roll(both_dot, queries, axis=1)
    slide_vec = jnp.zeros((here_tiles, lanes), jnp.int32)
    for tile in range(here_tiles):
        slide_vec = jnp.where(sub == tile, slide_ref[tile], slide_vec)
    valid = sub < valid_ref[0]
    members = [(slide_vec == slide) & valid for slide in range(slides)]
    for slide in range(slides):
        top = jnp.max(jnp.where(members[slide], scores, -1e30), axis=0, keepdims=True)
        weight = jnp.where(members[slide], jnp.exp(jnp.where(members[slide], scores - top, 0.0)), 0.0)
        total = jnp.sum(weight, axis=0, keepdims=True)
        dots = jnp.sum(weight * class_dot, axis=0, keepdims=True)
        part[slide:slide + 1, :] = jnp.where(first[:1], top, pltpu.roll(total, queries, axis=1))
        part[slides + slide:slides + slide + 1, :] = jnp.where(first[:1], dots, 0.0)

    pl.semaphore_wait(barrier, count - 1)

    def part_copy(hop, slot):
        return pltpu.make_async_remote_copy(
            src_ref=part, dst_ref=parts_all.at[slot], send_sem=part_send.at[hop], recv_sem=part_recv.at[hop],
            device_id={"tile": wrapped(me + hop)}, device_id_type=MESH)

    @pl.loop(1, count)
    def _(hop):
        part_copy(hop, me).start()

    parts_all[me] = part[...]

    @pl.loop(0, out_blocks)
    def _(at):
        cols = pl.ds(pl.multiple_of(at * WIDE, WIDE), WIDE)
        x_turned[cols, :] = x[:, cols].T

    @pl.loop(1, count)
    def _(hop):
        part_copy(hop, wrapped(me - hop + count)).wait_recv()

    gathered = parts_all[...]
    tops = jnp.max(gathered, axis=0)
    rescale = jnp.exp(gathered - tops[None])
    totals = jnp.sum(rescale * pltpu.roll(gathered, queries, axis=2), axis=0)
    ratio = jnp.sum(rescale * pltpu.roll(gathered, slides, axis=1), axis=0) / totals
    used = first & (sub < slides)
    logit = jnp.sum(jnp.where(used, ratio, 0.0), axis=1, keepdims=True) + jnp.zeros((here_tiles, lanes), f32)
    target_vec = jnp.zeros((here_tiles, lanes), jnp.int32)
    for slide in range(slides):
        target_vec = jnp.where(sub == slide, label_ref[slide], target_vec)
    targets = target_vec.astype(f32)
    loss_ref[...] = jnp.maximum(logit, 0.0) + jnp.log1p(jnp.exp(-jnp.abs(logit))) - targets * logit
    dlogit = (jax.nn.sigmoid(logit) - targets) * (1.0 / slides)

    def per_tile(values):
        result = jnp.zeros((here_tiles, lanes), f32)
        for slide in range(slides):
            result = jnp.where(members[slide], values[slide:slide + 1, :], result)
        return result

    live = valid & first
    weights = jnp.where(live, jnp.exp(jnp.where(live, scores - per_tile(tops), 0.0)), 0.0)
    prob_grad = jnp.where(live, weights / jnp.where(live, per_tile(totals), 1.0) * per_tile(dlogit), 0.0)
    dscore = jnp.where(live, prob_grad * (class_dot - per_tile(ratio)), 0.0) * inv_root
    coef = dscore + pltpu.roll(prob_grad, queries, axis=1)
    dembed3 = jnp.dot(jnp.concatenate(three_pieces(coef), axis=0).astype(jnp.bfloat16), both[...],
                      preferred_element_type=f32)
    embed[...] = (dembed3[:here_tiles] + dembed3[here_tiles:2 * here_tiles] + dembed3[2 * here_tiles:]) * (1.0 / positions)

    partners = [me + (1 << bit) * (1 - 2 * ((me // (1 << bit)) % 2)) for bit in range(steps)]

    def span(order, step, unit):
        half = count >> (step + 1)
        base = 0
        for at in range(step):
            base = base + ((me // (1 << order[at])) % 2) * (count >> (at + 1))
        mine = (me // (1 << order[step])) % 2
        keep = pl.multiple_of((base + mine * half) * unit, unit)
        give = pl.multiple_of((base + (1 - mine) * half) * unit, unit)
        return keep, give, half * unit

    def land_at(step, unit):
        return (count - (count >> step)) * unit

    def begin(source, land, order, step, unit, sends, recvs):
        keep, give, size = span(order, step, unit)
        copy = pltpu.make_async_remote_copy(
            src_ref=source.at[pl.ds(give, size)],
            dst_ref=land.at[pl.ds(land_at(step, unit), size)],
            send_sem=sends, recv_sem=recvs,
            device_id={"tile": partners[order[step]]},
            device_id_type=MESH,
        )
        copy.start()
        return copy

    def add(source, land, order, step, unit):
        keep, give, size = span(order, step, unit)
        piece = min(size, 256)

        @pl.loop(0, size // piece)
        def _(at):
            here = pl.ds(pl.multiple_of(keep + at * piece, piece), piece)
            there = pl.ds(pl.multiple_of(land_at(step, unit) + at * piece, piece), piece)
            source[here, :] = source[here, :] + land[there, :]

    copies = {}

    def send(step, chunk):
        copies[step, chunk] = begin(grads[chunk], lands[chunk], orders[chunk], step, unit_rows,
                                    send_sem.at[step, chunk], recv_sem.at[step, chunk])

    query_order = list(range(steps))
    query_copies = []

    def query_start():
        terms = three_pieces(dscore)
        sides = three_pieces(embeds)
        left = jnp.concatenate([terms[0], terms[0], terms[1], terms[1], terms[0], terms[2]], axis=0)
        right = jnp.concatenate([sides[0], sides[1], sides[0], sides[1], sides[2], sides[0]], axis=0)
        product = lax.dot_general(left.astype(jnp.bfloat16), right.astype(jnp.bfloat16), (((0,), (0,)), ((), ())),
                                  preferred_element_type=f32)
        for above in range(queries // 8):
            for beside in range(width // 128):
                at = (above * (width // 128) + beside) * 8
                query_sum[at:at + 8, :] = product[above * 8:above * 8 + 8, beside * 128:beside * 128 + 128]
        query_copies.append(begin(query_sum, query_land, query_order, 0, query_rows,
                                  query_send.at[0], query_recv.at[0]))

    def share(step):
        keep, give, size = span(query_order, step, query_rows)
        held = query_full.at[pl.ds(keep, size)]
        copy = pltpu.make_async_remote_copy(
            src_ref=held, dst_ref=held,
            send_sem=query_send.at[steps + step], recv_sem=query_recv.at[steps + step],
            device_id={"tile": partners[query_order[step]]},
            device_id_type=MESH,
        )
        copy.start()
        return copy

    def advance_query():
        done = len(query_copies) - 1
        query_copies[done].wait()
        if done < steps:
            add(query_sum, query_land, query_order, done, query_rows)
        if done < steps - 1:
            query_copies.append(begin(query_sum, query_land, query_order, done + 1, query_rows,
                                      query_send.at[done + 1], query_recv.at[done + 1]))
            return
        if done == steps - 1:
            own = pl.ds(pl.multiple_of(place_of(me, query_order) * query_rows, query_rows), query_rows)
            query_full[own, :] = query_sum[own, :]
        query_copies.append(share(2 * steps - 2 - done) if done < 2 * steps - 1 else None)

    query_start()
    for at in range(out_blocks):
        cols = slice(at * WIDE, (at + 1) * WIDE)
        block = jnp.concatenate(
            [slope_out[tile * positions:(tile + 1) * positions, cols] * embed[tile:tile + 1, cols]
             for tile in range(here_tiles)], axis=0).astype(jnp.bfloat16)
        dout[:, cols] = block
        dout_turned[cols, :] = block.T

    def multiply(left, right, right_cols, chunk):
        for at in range(width // TALL):
            product = jnp.dot(left[at * TALL:(at + 1) * TALL, :], right[:, right_cols], preferred_element_type=f32)
            for inner in range(TALL // rows):
                for part in range(per_block):
                    side, half = part // SPLIT, part % SPLIT
                    place = place_of(at * (TALL // rows) + inner, orders[chunk + part]) * unit_rows
                    start = inner * rows + half * unit_rows
                    grads[chunk + part][place:place + unit_rows, :] = product[
                        start:start + unit_rows, side * CHUNK:(side + 1) * CHUNK]

    def produce(chunk):
        first_col = chunk % per_matrix // per_block * WIDE
        cols = slice(first_col, first_col + WIDE)
        if chunk < per_matrix:
            multiply(dout_turned, hidden, cols, chunk)
        else:
            dmid = lax.dot_general(dout[...], we[cols, :], (((1,), (1,)), ((), ())), preferred_element_type=f32)
            dpre[...] = (dmid * slope_mid[:, cols]).astype(jnp.bfloat16)
            multiply(x_turned, dpre, slice(0, WIDE), chunk)
        for part in range(per_block):
            send(0, chunk + part)

    for code in order_of_steps:
        chunk, step = code // 16, code % 16
        if code < 0:
            produce((-1 - code) * per_block)
            continue
        if chunk == chunks:
            advance_query()
            continue
        order = orders[chunk]
        copies[step - 1, chunk].wait()
        add(grads[chunk], lands[chunk], order, step - 1, unit_rows)
        if step < steps:
            send(step, chunk)
        else:
            out_ref = (exp_ref, red_ref)[chunk // per_matrix]
            start = chunk % per_matrix // SPLIT * CHUNK
            top = chunk % SPLIT * unit_rows
            out_ref[top:top + unit_rows, start:start + CHUNK] = grads[chunk][
                pl.ds(pl.multiple_of(place_of(me, order) * unit_rows, unit_rows), unit_rows), :
            ]
    for above in range(queries // 8):
        for beside in range(width // 128):
            at = (above * (width // 128) + beside) * 8
            query_out_ref[above * 8:above * 8 + 8, beside * 128:beside * 128 + 128] = query_full[at:at + 8, :]

    @pl.loop(1, count)
    def _(hop):
        part_copy(hop, me).wait_send()


def hand_over_kernel(red_in, exp_in, query_in, loss_in, loss_out, query_out, red_out, exp_out, *scratch):
    buffers, (in_sems, out_sems) = scratch[:3], scratch[3:]
    pairs = ((query_in, query_out), (red_in, red_out), (exp_in, exp_out))
    loads = [pltpu.make_async_copy(pair[0], buffers[at], in_sems.at[at]) for at, pair in enumerate(pairs)]
    stores = [pltpu.make_async_copy(buffers[at], pair[1], out_sems.at[at]) for at, pair in enumerate(pairs)]
    for load in loads:
        load.start()
    for slide in range(loss_out.shape[0]):
        loss_out[slide] = loss_in[slide, 0]
    for load, store in zip(loads, stores):
        load.wait()
        store.start()
    for store in stores:
        store.wait()


def on_device(count, tiles, slide_of, valid_count, labels, w_reduce, w_expand, queries, cls_weight):
    here_tiles, positions, width = tiles.shape
    slides = labels.shape[0]
    middle = w_reduce.shape[1]
    count_queries = queries.shape[0]
    rows_here = here_tiles * positions
    orders, order_of_steps = plan_of(count, 2 * middle // WIDE)
    steps = len(orders[0])
    chunks = len(orders)
    lanes = 2 * count_queries
    vmem = pl.BlockSpec(memory_space=pltpu.VMEM)
    smem = pl.BlockSpec(memory_space=pltpu.SMEM)
    anywhere = pl.BlockSpec(memory_space=pl.ANY)
    f32, bf16 = jnp.float32, jnp.bfloat16
    flat = (count_queries * width // 128, 128)
    red, exp, shared, loss = pl.pallas_call(
        functools.partial(step_kernel, count, slides, positions, orders, order_of_steps),
        out_shape=(
            jax.ShapeDtypeStruct((width // count, middle), f32),
            jax.ShapeDtypeStruct((width // count, middle), f32),
            jax.ShapeDtypeStruct((count_queries, width), f32),
            jax.ShapeDtypeStruct((here_tiles, lanes), f32),
        ),
        in_specs=[anywhere] * 8,
        out_specs=(vmem,) * 4,
        scratch_shapes=(
            [pltpu.VMEM((width // SPLIT, CHUNK), f32)] * (2 * chunks)
            + [
                pltpu.VMEM((rows_here, width), bf16),
                pltpu.VMEM((width, middle), bf16),
                pltpu.VMEM((middle, width), bf16),
                pltpu.VMEM((lanes, width), bf16),
                pltpu.VMEM((rows_here, middle), bf16),
                pltpu.VMEM((rows_here, middle), f32),
                pltpu.VMEM((rows_here, width), f32),
                pltpu.VMEM((rows_here, width), bf16),
                pltpu.VMEM((width, rows_here), bf16),
                pltpu.VMEM((width, rows_here), bf16),
                pltpu.VMEM((rows_here, WIDE), bf16),
                pltpu.VMEM((here_tiles, width), f32),
                pltpu.VMEM((here_tiles, lanes), f32),
                pltpu.VMEM((count, here_tiles, lanes), f32),
                pltpu.SMEM(slide_of.shape, jnp.int32),
                pltpu.SMEM(valid_count.shape, jnp.int32),
                pltpu.SMEM(labels.shape, jnp.int32),
                pltpu.VMEM(flat, f32),
                pltpu.VMEM(flat, f32),
                pltpu.VMEM(flat, f32),
                pltpu.SemaphoreType.DMA((7 + middle // WIDE,)),
                pltpu.SemaphoreType.DMA((count,)),
                pltpu.SemaphoreType.DMA((count,)),
                pltpu.SemaphoreType.DMA((steps, chunks)),
                pltpu.SemaphoreType.DMA((steps, chunks)),
                pltpu.SemaphoreType.DMA((2 * steps,)),
                pltpu.SemaphoreType.DMA((2 * steps,)),
            ]
        ),
        compiler_params=pltpu.CompilerParams(
            collective_id=0, has_side_effects=True, vmem_limit_bytes=62 * 1024 * 1024
        ),
    )(slide_of, valid_count, labels, tiles.reshape(rows_here, width), w_reduce, w_expand, queries, cls_weight)
    return pl.pallas_call(
        hand_over_kernel,
        out_shape=(
            jax.ShapeDtypeStruct((slides,), f32),
            jax.ShapeDtypeStruct(shared.shape, f32),
            jax.ShapeDtypeStruct(red.shape, f32),
            jax.ShapeDtypeStruct(exp.shape, f32),
        ),
        in_specs=[anywhere] * 3 + [vmem],
        out_specs=(smem,) + (anywhere,) * 3,
        scratch_shapes=[pltpu.VMEM(value.shape, f32) for value in (shared, red, exp)]
        + [pltpu.SemaphoreType.DMA((3,)), pltpu.SemaphoreType.DMA((3,))],
    )(red, exp, shared, loss)


def solution(mesh):
    return jax.shard_map(
        functools.partial(on_device, mesh.shape["tile"]),
        mesh=mesh,
        in_specs=(
            P(("groups", "tile"), None, None),
            P(("groups", "tile")),
            P(("groups", "tile")),
            P("groups"),
            P(),
            P(),
            P(),
            P(),
        ),
        out_specs=(
            P("groups"),
            P("groups", None),
            P(("groups", "tile"), None),
            P(("groups", "tile"), None),
        ),
        check_vma=False,
    )
```

```python
import functools

import jax
import jax.numpy as jnp
import numpy as np
from jax import lax
from jax.experimental import pallas as pl
from jax.experimental.pallas import tpu as pltpu
from jax.sharding import PartitionSpec as P

CHUNK = 128
WIDE = 256
TALL = 512
LAG = 4
SPLIT = 1
KINDS = (
    2, 0, 1, 2, 0, 2, 0, 1, 0, 1, 1, 2, 0, 0, 1, 1,
)
STEPS = (
    -1, 257, -2, 1, -3, 17, 33, -4, -5, 81, 97, 113, 258, 65, -6, 129, 2, 34, 49, 161, 98, -7, 193, 114,
    259, 82, 66, 177, 145, -8, 50, 18, 130, 99, 162, 260, 67, 35, 178, 146, 194, 209, 51, 115, 241, 261, 19, 225,
    36, 163, 100, 262, 20, 242, 68, 116, 147, 131, 179, 52, 263, 195, 210, 164, 69, 101, 226, 243, 3, 83, 132, 148,
    196, 180, 227, 53, 21, 211, 37, 244, 4, 181, 264, 117, 133, 228, 84, 212, 265, 165, 245, 85, 5, 197, 229, 149,
    266, 213,
)
MESH = pl.DeviceIdType.MESH


def plan_of(count, blocks):
    bits = count.bit_length() - 1
    parts = blocks * (WIDE // CHUNK) * SPLIT
    if (bits, blocks) == (5, 8):
        orders = [[0, 1, 2, 3, 4], [0, 2, 1, 3, 4], [0, 3, 4, 1, 2]]
        return [orders[kind] for kind in KINDS], STEPS
    ring = list(range(1, bits))
    turns = [ring[turn:] + ring[:turn] for turn in (0, 1, 2)]
    orders = [[0] + turns[part // SPLIT % 8 % 3] for part in range(parts)]
    per_block = parts // blocks
    keyed = []
    for part in range(parts):
        if part % per_block == 0:
            keyed.append((part / SPLIT, -1 - part // per_block))
        for step in range(1, bits + 1):
            keyed.append((part / SPLIT + LAG * step, part * 16 + step))
    for step in range(1, 2 * bits + 1):
        keyed.append((step * 0.5 * LAG, parts * 16 + step))
    return orders, [code for key, code in sorted(keyed, key=lambda pair: pair[0])]


def place_of(block, order):
    place = 0
    for bit in order:
        place = place * 2 + (block // (1 << bit)) % 2
    return place


def three_pieces(values):
    high = values.astype(jnp.bfloat16).astype(jnp.float32)
    rest = values - high
    middle = rest.astype(jnp.bfloat16).astype(jnp.float32)
    return high, middle, rest - middle


def step_kernel(count, slides, positions, orders, order_of_steps, slide_any, valid_any, label_any, tiles_ref, reduce_ref, expand_ref,
                query_ref, class_ref, red_ref, exp_ref, query_out_ref, loss_ref, *scratch):
    width, middle = reduce_ref.shape
    rows_here = tiles_ref.shape[0]
    here_tiles = rows_here // positions
    queries = query_ref.shape[0]
    lanes = 2 * queries
    per_matrix = middle // CHUNK * SPLIT
    per_block = WIDE // CHUNK * SPLIT
    chunks = 2 * per_matrix
    grads = scratch[:chunks]
    lands = scratch[chunks:2 * chunks]
    (x, wr, we, both, hidden, slope_mid, slope_out, dout, dpre, embed, part, parts_all, slide_ref, valid_ref, label_ref,
     query_sum, query_land, query_full, load_sem, part_send, part_recv, send_sem, recv_sem, query_send, query_recv,
     ) = scratch[2 * chunks:]
    steps = len(orders[0])
    me = lax.axis_index("tile")
    turned = [wr.at[:, pl.ds(side * rows_here, rows_here)] for side in (0, 1)]
    x_turned, dout_turned = turned
    rows = width // count
    unit_rows = rows // SPLIT
    query_rows = query_sum.shape[0] // count
    inv_root = np.float32(1.0) / np.sqrt(np.float32(width))
    f32 = jnp.float32

    barrier = pltpu.get_barrier_semaphore()

    mid_blocks = middle // WIDE
    out_blocks = width // WIDE
    def load(source, target, at):
        copy = pltpu.make_async_copy(source, target, load_sem.at[at])
        copy.start()
        return copy
    def columns(ref, at):
        return ref.at[:, pl.ds(at * WIDE, WIDE)]
    x_load = load(tiles_ref, x, 0)
    for at in range(mid_blocks):
        load(columns(reduce_ref, at), columns(wr, at), 4 + at)
    we_load = load(expand_ref, we, 1)
    both_loads = [load(query_ref, both.at[pl.ds(0, queries)], 2), load(class_ref, both.at[pl.ds(queries, queries)], 3)]

    small_loads = [load(slide_any, slide_ref, 4 + mid_blocks), load(valid_any, valid_ref, 5 + mid_blocks),
                   load(label_any, label_ref, 6 + mid_blocks)]

    def wrapped(device):
        return jnp.where(device >= count, device - count, device)

    @pl.loop(1, count)
    def _(hop):
        pl.semaphore_signal(barrier, inc=1, device_id={"tile": wrapped(me + hop)}, device_id_type=MESH)

    x_load.wait()

    @pl.loop(0, mid_blocks)
    def _(at):
        cols = pl.ds(pl.multiple_of(at * WIDE, WIDE), WIDE)
        pltpu.make_async_copy(reduce_ref.at[:, cols], wr.at[:, cols], load_sem.at[4 + at]).wait()
        pre = jnp.dot(x[...], wr[:, cols], preferred_element_type=f32)
        sig = 0.5 * jnp.tanh(0.5 * pre) + 0.5
        act = pre * sig
        hidden[:, cols] = act.astype(jnp.bfloat16)
        slope_mid[:, cols] = sig + act * (1.0 - sig)
    we_load.wait()

    @pl.loop(0, width // TALL)
    def _(at):
        cols = pl.ds(pl.multiple_of(at * TALL, TALL), TALL)
        pre = x[:, cols].astype(f32) + jnp.dot(hidden[...], we[:, cols], preferred_element_type=f32)
        sig = 0.5 * jnp.tanh(0.5 * pre) + 0.5
        act = pre * sig
        slope_out[:, cols] = sig + act * (1.0 - sig)
        embed[:, cols] = jnp.sum(act.reshape(here_tiles, positions, TALL), axis=1) * (1.0 / positions)

    for copy in both_loads + small_loads:
        copy.wait()

    embeds = embed[...]
    pieces = three_pieces(embeds)
    score3 = lax.dot_general(jnp.concatenate(pieces, axis=0).astype(jnp.bfloat16), both[...],
                             (((1,), (1,)), ((), ())), preferred_element_type=f32)
    both_dot = score3[:here_tiles] + score3[here_tiles:2 * here_tiles] + score3[2 * here_tiles:]
    sub = lax.broadcasted_iota(jnp.int32, (here_tiles, lanes), 0)
    lane = lax.broadcasted_iota(jnp.int32, (here_tiles, lanes), 1)
    first = lane < queries
    scores = both_dot * inv_root
    class_dot = pltpu.roll(both_dot, queries, axis=1)
    slide_vec = jnp.zeros((here_tiles, lanes), jnp.int32)
    for tile in range(here_tiles):
        slide_vec = jnp.where(sub == tile, slide_ref[tile], slide_vec)
    valid = sub < valid_ref[0]
    members = [(slide_vec == slide) & valid for slide in range(slides)]
    for slide in range(slides):
        top = jnp.max(jnp.where(members[slide], scores, -1e30), axis=0, keepdims=True)
        weight = jnp.where(members[slide], jnp.exp(jnp.where(members[slide], scores - top, 0.0)), 0.0)
        total = jnp.sum(weight, axis=0, keepdims=True)
        dots = jnp.sum(weight * class_dot, axis=0, keepdims=True)
        part[slide:slide + 1, :] = jnp.where(first[:1], top, pltpu.roll(total, queries, axis=1))
        part[slides + slide:slides + slide + 1, :] = jnp.where(first[:1], dots, 0.0)

    pl.semaphore_wait(barrier, count - 1)

    def part_copy(hop, slot):
        return pltpu.make_async_remote_copy(
            src_ref=part, dst_ref=parts_all.at[slot], send_sem=part_send.at[hop], recv_sem=part_recv.at[hop],
            device_id={"tile": wrapped(me + hop)}, device_id_type=MESH)

    @pl.loop(1, count)
    def _(hop):
        part_copy(hop, me).start()

    parts_all[me] = part[...]

    @pl.loop(0, out_blocks)
    def _(at):
        cols = pl.ds(pl.multiple_of(at * WIDE, WIDE), WIDE)
        x_turned[cols, :] = x[:, cols].T

    @pl.loop(1, count)
    def _(hop):
        part_copy(hop, wrapped(me - hop + count)).wait_recv()

    gathered = parts_all[...]
    tops = jnp.max(gathered, axis=0)
    rescale = jnp.exp(gathered - tops[None])
    totals = jnp.sum(rescale * pltpu.roll(gathered, queries, axis=2), axis=0)
    ratio = jnp.sum(rescale * pltpu.roll(gathered, slides, axis=1), axis=0) / totals
    used = first & (sub < slides)
    logit = jnp.sum(jnp.where(used, ratio, 0.0), axis=1, keepdims=True) + jnp.zeros((here_tiles, lanes), f32)
    target_vec = jnp.zeros((here_tiles, lanes), jnp.int32)
    for slide in range(slides):
        target_vec = jnp.where(sub == slide, label_ref[slide], target_vec)
    targets = target_vec.astype(f32)
    loss_ref[...] = jnp.maximum(logit, 0.0) + jnp.log1p(jnp.exp(-jnp.abs(logit))) - targets * logit
    dlogit = (jax.nn.sigmoid(logit) - targets) * (1.0 / slides)

    def per_tile(values):
        result = jnp.zeros((here_tiles, lanes), f32)
        for slide in range(slides):
            result = jnp.where(members[slide], values[slide:slide + 1, :], result)
        return result

    live = valid & first
    weights = jnp.where(live, jnp.exp(jnp.where(live, scores - per_tile(tops), 0.0)), 0.0)
    prob_grad = jnp.where(live, weights / jnp.where(live, per_tile(totals), 1.0) * per_tile(dlogit), 0.0)
    dscore = jnp.where(live, prob_grad * (class_dot - per_tile(ratio)), 0.0) * inv_root
    coef = dscore + pltpu.roll(prob_grad, queries, axis=1)
    dembed3 = jnp.dot(jnp.concatenate(three_pieces(coef), axis=0).astype(jnp.bfloat16), both[...],
                      preferred_element_type=f32)
    embed[...] = (dembed3[:here_tiles] + dembed3[here_tiles:2 * here_tiles] + dembed3[2 * here_tiles:]) * (1.0 / positions)

    partners = [me + (1 << bit) * (1 - 2 * ((me // (1 << bit)) % 2)) for bit in range(steps)]

    def span(order, step, unit):
        half = count >> (step + 1)
        base = 0
        for at in range(step):
            base = base + ((me // (1 << order[at])) % 2) * (count >> (at + 1))
        mine = (me // (1 << order[step])) % 2
        keep = pl.multiple_of((base + mine * half) * unit, unit)
        give = pl.multiple_of((base + (1 - mine) * half) * unit, unit)
        return keep, give, half * unit

    def land_at(step, unit):
        return (count - (count >> step)) * unit

    def begin(source, land, order, step, unit, sends, recvs):
        keep, give, size = span(order, step, unit)
        copy = pltpu.make_async_remote_copy(
            src_ref=source.at[pl.ds(give, size)],
            dst_ref=land.at[pl.ds(land_at(step, unit), size)],
            send_sem=sends, recv_sem=recvs,
            device_id={"tile": partners[order[step]]},
            device_id_type=MESH,
        )
        copy.start()
        return copy

    def add(source, land, order, step, unit):
        keep, give, size = span(order, step, unit)
        piece = min(size, 256)

        @pl.loop(0, size // piece)
        def _(at):
            here = pl.ds(pl.multiple_of(keep + at * piece, piece), piece)
            there = pl.ds(pl.multiple_of(land_at(step, unit) + at * piece, piece), piece)
            source[here, :] = source[here, :] + land[there, :]

    copies = {}

    def send(step, chunk):
        copies[step, chunk] = begin(grads[chunk], lands[chunk], orders[chunk], step, unit_rows,
                                    send_sem.at[step, chunk], recv_sem.at[step, chunk])

    query_order = list(range(steps))
    query_copies = []

    def query_start():
        terms = three_pieces(dscore)
        sides = three_pieces(embeds)
        left = jnp.concatenate([terms[0], terms[0], terms[1], terms[1], terms[0], terms[2]], axis=0)
        right = jnp.concatenate([sides[0], sides[1], sides[0], sides[1], sides[2], sides[0]], axis=0)
        product = lax.dot_general(left.astype(jnp.bfloat16), right.astype(jnp.bfloat16), (((0,), (0,)), ((), ())),
                                  preferred_element_type=f32)
        for above in range(queries // 8):
            for beside in range(width // 128):
                at = (above * (width // 128) + beside) * 8
                query_sum[at:at + 8, :] = product[above * 8:above * 8 + 8, beside * 128:beside * 128 + 128]
        query_copies.append(begin(query_sum, query_land, query_order, 0, query_rows,
                                  query_send.at[0], query_recv.at[0]))

    def share(step):
        keep, give, size = span(query_order, step, query_rows)
        held = query_full.at[pl.ds(keep, size)]
        copy = pltpu.make_async_remote_copy(
            src_ref=held, dst_ref=held,
            send_sem=query_send.at[steps + step], recv_sem=query_recv.at[steps + step],
            device_id={"tile": partners[query_order[step]]},
            device_id_type=MESH,
        )
        copy.start()
        return copy

    def advance_query():
        done = len(query_copies) - 1
        query_copies[done].wait()
        if done < steps:
            add(query_sum, query_land, query_order, done, query_rows)
        if done < steps - 1:
            query_copies.append(begin(query_sum, query_land, query_order, done + 1, query_rows,
                                      query_send.at[done + 1], query_recv.at[done + 1]))
            return
        if done == steps - 1:
            own = pl.ds(pl.multiple_of(place_of(me, query_order) * query_rows, query_rows), query_rows)
            query_full[own, :] = query_sum[own, :]
        query_copies.append(share(2 * steps - 2 - done) if done < 2 * steps - 1 else None)

    query_start()
    for at in range(out_blocks):
        cols = slice(at * WIDE, (at + 1) * WIDE)
        block = jnp.concatenate(
            [slope_out[tile * positions:(tile + 1) * positions, cols] * embed[tile:tile + 1, cols]
             for tile in range(here_tiles)], axis=0).astype(jnp.bfloat16)
        dout[:, cols] = block
        dout_turned[cols, :] = block.T

    def multiply(left, right, right_cols, chunk):
        for at in range(width // TALL):
            product = jnp.dot(left[at * TALL:(at + 1) * TALL, :], right[:, right_cols], preferred_element_type=f32)
            for inner in range(TALL // rows):
                for part in range(per_block):
                    side, half = part // SPLIT, part % SPLIT
                    place = place_of(at * (TALL // rows) + inner, orders[chunk + part]) * unit_rows
                    start = inner * rows + half * unit_rows
                    grads[chunk + part][place:place + unit_rows, :] = product[
                        start:start + unit_rows, side * CHUNK:(side + 1) * CHUNK]

    def produce(chunk):
        first_col = chunk % per_matrix // per_block * WIDE
        cols = slice(first_col, first_col + WIDE)
        if chunk < per_matrix:
            multiply(dout_turned, hidden, cols, chunk)
        else:
            dmid = lax.dot_general(dout[...], we[cols, :], (((1,), (1,)), ((), ())), preferred_element_type=f32)
            dpre[...] = (dmid * slope_mid[:, cols]).astype(jnp.bfloat16)
            multiply(x_turned, dpre, slice(0, WIDE), chunk)
        for part in range(per_block):
            send(0, chunk + part)

    for code in order_of_steps:
        chunk, step = code // 16, code % 16
        if code < 0:
            produce((-1 - code) * per_block)
            continue
        if chunk == chunks:
            advance_query()
            continue
        order = orders[chunk]
        copies[step - 1, chunk].wait()
        add(grads[chunk], lands[chunk], order, step - 1, unit_rows)
        if step < steps:
            send(step, chunk)
        else:
            out_ref = (exp_ref, red_ref)[chunk // per_matrix]
            start = chunk % per_matrix // SPLIT * CHUNK
            top = chunk % SPLIT * unit_rows
            out_ref[top:top + unit_rows, start:start + CHUNK] = grads[chunk][
                pl.ds(pl.multiple_of(place_of(me, order) * unit_rows, unit_rows), unit_rows), :
            ]
    for above in range(queries // 8):
        for beside in range(width // 128):
            at = (above * (width // 128) + beside) * 8
            query_out_ref[above * 8:above * 8 + 8, beside * 128:beside * 128 + 128] = query_full[at:at + 8, :]

    @pl.loop(1, count)
    def _(hop):
        part_copy(hop, me).wait_send()


def hand_over_kernel(red_in, exp_in, query_in, loss_in, loss_out, query_out, red_out, exp_out, sems):
    copies = [
        pltpu.make_async_copy(source, target, sems.at[at])
        for at, (source, target) in enumerate(((query_in, query_out), (red_in, red_out), (exp_in, exp_out)))
    ]
    for copy in copies:
        copy.start()
    for slide in range(loss_out.shape[0]):
        loss_out[slide] = loss_in[slide, 0]
    for copy in copies:
        copy.wait()


def on_device(count, tiles, slide_of, valid_count, labels, w_reduce, w_expand, queries, cls_weight):
    here_tiles, positions, width = tiles.shape
    slides = labels.shape[0]
    middle = w_reduce.shape[1]
    count_queries = queries.shape[0]
    rows_here = here_tiles * positions
    orders, order_of_steps = plan_of(count, 2 * middle // WIDE)
    steps = len(orders[0])
    chunks = len(orders)
    lanes = 2 * count_queries
    vmem = pl.BlockSpec(memory_space=pltpu.VMEM)
    smem = pl.BlockSpec(memory_space=pltpu.SMEM)
    anywhere = pl.BlockSpec(memory_space=pl.ANY)
    f32, bf16 = jnp.float32, jnp.bfloat16
    flat = (count_queries * width // 128, 128)
    red, exp, shared, loss = pl.pallas_call(
        functools.partial(step_kernel, count, slides, positions, orders, order_of_steps),
        out_shape=(
            pltpu.VMEM((width // count, middle), f32),
            pltpu.VMEM((width // count, middle), f32),
            pltpu.VMEM((count_queries, width), f32),
            pltpu.VMEM((here_tiles, lanes), f32),
        ),
        in_specs=[anywhere] * 8,
        out_specs=(vmem,) * 4,
        scratch_shapes=(
            [pltpu.VMEM((width // SPLIT, CHUNK), f32)] * (2 * chunks)
            + [
                pltpu.VMEM((rows_here, width), bf16),
                pltpu.VMEM((width, middle), bf16),
                pltpu.VMEM((middle, width), bf16),
                pltpu.VMEM((lanes, width), bf16),
                pltpu.VMEM((rows_here, middle), bf16),
                pltpu.VMEM((rows_here, middle), f32),
                pltpu.VMEM((rows_here, width), f32),
                pltpu.VMEM((rows_here, width), bf16),
                pltpu.VMEM((rows_here, WIDE), bf16),
                pltpu.VMEM((here_tiles, width), f32),
                pltpu.VMEM((here_tiles, lanes), f32),
                pltpu.VMEM((count, here_tiles, lanes), f32),
                pltpu.SMEM(slide_of.shape, jnp.int32),
                pltpu.SMEM(valid_count.shape, jnp.int32),
                pltpu.SMEM(labels.shape, jnp.int32),
                pltpu.VMEM(flat, f32),
                pltpu.VMEM(flat, f32),
                pltpu.VMEM(flat, f32),
                pltpu.SemaphoreType.DMA((7 + middle // WIDE,)),
                pltpu.SemaphoreType.DMA((count,)),
                pltpu.SemaphoreType.DMA((count,)),
                pltpu.SemaphoreType.DMA((steps, chunks)),
                pltpu.SemaphoreType.DMA((steps, chunks)),
                pltpu.SemaphoreType.DMA((2 * steps,)),
                pltpu.SemaphoreType.DMA((2 * steps,)),
            ]
        ),
        compiler_params=pltpu.CompilerParams(
            collective_id=0, has_side_effects=True, vmem_limit_bytes=60 * 1024 * 1024
        ),
    )(slide_of, valid_count, labels, tiles.reshape(rows_here, width), w_reduce, w_expand, queries, cls_weight)
    held = [pltpu.with_memory_space_constraint(value, pltpu.VMEM) for value in (red, exp, shared, loss)]
    return pl.pallas_call(
        hand_over_kernel,
        out_shape=(
            jax.ShapeDtypeStruct((slides,), f32),
            jax.ShapeDtypeStruct(shared.shape, f32),
            jax.ShapeDtypeStruct(red.shape, f32),
            jax.ShapeDtypeStruct(exp.shape, f32),
        ),
        in_specs=[vmem] * 4,
        out_specs=(smem,) + (anywhere,) * 3,
        scratch_shapes=[pltpu.SemaphoreType.DMA((3,))],
    )(*held)


def solution(mesh):
    return jax.shard_map(
        functools.partial(on_device, mesh.shape["tile"]),
        mesh=mesh,
        in_specs=(
            P(("groups", "tile"), None, None),
            P(("groups", "tile")),
            P(("groups", "tile")),
            P("groups"),
            P(),
            P(),
            P(),
            P(),
        ),
        out_specs=(
            P("groups"),
            P("groups", None),
            P(("groups", "tile"), None),
            P(("groups", "tile"), None),
        ),
        check_vma=False,
    )
```

```python
import functools

import jax
import jax.numpy as jnp
import numpy as np
from jax import lax
from jax.experimental import pallas as pl
from jax.experimental.pallas import tpu as pltpu
from jax.sharding import PartitionSpec as P

CHUNK = 128
WIDE = 256
TALL = 512
LAG = 4
SPLIT = 1
KINDS = (
    2, 0, 1, 2, 0, 2, 0, 1, 0, 1, 1, 2, 0, 0, 1, 1,
)
STEPS = (
    -1, 257, -2, 1, -3, 33, 17, 65, 81, 258, -4, -5, -6, 113, 259, 161, 2, 97, 177, -7, 34, -8, 260, 49,
    66, 114, 18, 98, 82, 145, 162, 35, 193, 19, 261, 241, 209, 99, 178, 194, 115, 67, 129, 50, 210, 163, 146, 262,
    68, 195, 225, 130, 242, 116, 83, 100, 3, 211, 20, 164, 196, 243, 147, 226, 263, 212, 36, 69, 4, 179, 51, 131,
    197, 101, 21, 244, 227, 264, 213, 84, 180, 148, 132, 37, 52, 117, 228, 265, 165, 181, 5, 245, 266, 53, 149, 85,
    133, 229,
)
MESH = pl.DeviceIdType.MESH


def plan_of(count, blocks):
    bits = count.bit_length() - 1
    parts = blocks * (WIDE // CHUNK) * SPLIT
    if (bits, blocks) == (5, 8):
        orders = [[0, 1, 2, 3, 4], [0, 2, 1, 3, 4], [0, 3, 4, 1, 2]]
        return [orders[kind] for kind in KINDS], STEPS
    ring = list(range(1, bits))
    turns = [ring[turn:] + ring[:turn] for turn in (0, 1, 2)]
    orders = [[0] + turns[part // SPLIT % 8 % 3] for part in range(parts)]
    per_block = parts // blocks
    keyed = []
    for part in range(parts):
        if part % per_block == 0:
            keyed.append((part / SPLIT, -1 - part // per_block))
        for step in range(1, bits + 1):
            keyed.append((part / SPLIT + LAG * step, part * 16 + step))
    for step in range(1, 2 * bits + 1):
        keyed.append((step * 0.5 * LAG, parts * 16 + step))
    return orders, [code for key, code in sorted(keyed, key=lambda pair: pair[0])]


def place_of(block, order):
    place = 0
    for bit in order:
        place = place * 2 + (block // (1 << bit)) % 2
    return place


def three_pieces(values):
    high = values.astype(jnp.bfloat16).astype(jnp.float32)
    rest = values - high
    middle = rest.astype(jnp.bfloat16).astype(jnp.float32)
    return high, middle, rest - middle


def step_kernel(count, slides, positions, orders, order_of_steps, slide_any, valid_any, label_any, tiles_ref, reduce_ref, expand_ref,
                query_ref, class_ref, red_ref, exp_ref, query_out_ref, loss_ref, *scratch):
    width, middle = reduce_ref.shape
    rows_here = tiles_ref.shape[0]
    here_tiles = rows_here // positions
    queries = query_ref.shape[0]
    lanes = 2 * queries
    per_matrix = middle // CHUNK * SPLIT
    per_block = WIDE // CHUNK * SPLIT
    chunks = 2 * per_matrix
    grads = scratch[:chunks]
    lands = scratch[chunks:2 * chunks]
    (x, wr, we, both, hidden, slope_mid, slope_out, dout, dpre, embed, part, parts_all, slide_ref, valid_ref, label_ref,
     query_sum, query_land, query_full, load_sem, part_send, part_recv, send_sem, recv_sem, query_send, query_recv,
     ) = scratch[2 * chunks:]
    steps = len(orders[0])
    me = lax.axis_index("tile")
    turned = [wr.at[:, pl.ds(side * rows_here, rows_here)] for side in (0, 1)]
    x_turned, dout_turned = turned
    rows = width // count
    unit_rows = rows // SPLIT
    query_rows = query_sum.shape[0] // count
    inv_root = np.float32(1.0) / np.sqrt(np.float32(width))
    f32 = jnp.float32

    barrier = pltpu.get_barrier_semaphore()

    mid_blocks = middle // WIDE
    out_blocks = width // WIDE
    def load(source, target, at):
        copy = pltpu.make_async_copy(source, target, load_sem.at[at])
        copy.start()
        return copy
    def columns(ref, at):
        return ref.at[:, pl.ds(at * WIDE, WIDE)]
    x_load = load(tiles_ref, x, 0)
    for at in range(mid_blocks):
        load(columns(reduce_ref, at), columns(wr, at), 4 + at)
    we_load = load(expand_ref, we, 1)
    both_loads = [load(query_ref, both.at[pl.ds(0, queries)], 2), load(class_ref, both.at[pl.ds(queries, queries)], 3)]

    small_loads = [load(slide_any, slide_ref, 4 + mid_blocks), load(valid_any, valid_ref, 5 + mid_blocks),
                   load(label_any, label_ref, 6 + mid_blocks)]

    def wrapped(device):
        return jnp.where(device >= count, device - count, device)

    @pl.loop(1, count)
    def _(hop):
        pl.semaphore_signal(barrier, inc=1, device_id={"tile": wrapped(me + hop)}, device_id_type=MESH)

    x_load.wait()

    @pl.loop(0, mid_blocks)
    def _(at):
        cols = pl.ds(pl.multiple_of(at * WIDE, WIDE), WIDE)
        pltpu.make_async_copy(reduce_ref.at[:, cols], wr.at[:, cols], load_sem.at[4 + at]).wait()
        pre = jnp.dot(x[...], wr[:, cols], preferred_element_type=f32)
        sig = 0.5 * jnp.tanh(0.5 * pre) + 0.5
        act = pre * sig
        hidden[:, cols] = act.astype(jnp.bfloat16)
        slope_mid[:, cols] = sig + act * (1.0 - sig)
    we_load.wait()

    @pl.loop(0, width // (2 * TALL))
    def _(at):
        cols = pl.ds(pl.multiple_of(at * 2 * TALL, 2 * TALL), 2 * TALL)
        pre = x[:, cols].astype(f32) + jnp.dot(hidden[...], we[:, cols], preferred_element_type=f32)
        sig = 0.5 * jnp.tanh(0.5 * pre) + 0.5
        act = pre * sig
        slope_out[:, cols] = sig + act * (1.0 - sig)
        embed[:, cols] = jnp.sum(act.reshape(here_tiles, positions, 2 * TALL), axis=1) * (1.0 / positions)

    for copy in both_loads + small_loads:
        copy.wait()

    embeds = embed[...]
    pieces = three_pieces(embeds)
    score3 = lax.dot_general(jnp.concatenate(pieces, axis=0).astype(jnp.bfloat16), both[...],
                             (((1,), (1,)), ((), ())), preferred_element_type=f32)
    both_dot = score3[:here_tiles] + score3[here_tiles:2 * here_tiles] + score3[2 * here_tiles:]
    sub = lax.broadcasted_iota(jnp.int32, (here_tiles, lanes), 0)
    lane = lax.broadcasted_iota(jnp.int32, (here_tiles, lanes), 1)
    first = lane < queries
    scores = both_dot * inv_root
    class_dot = pltpu.roll(both_dot, queries, axis=1)
    slide_vec = jnp.zeros((here_tiles, lanes), jnp.int32)
    for tile in range(here_tiles):
        slide_vec = jnp.where(sub == tile, slide_ref[tile], slide_vec)
    valid = sub < valid_ref[0]
    members = [(slide_vec == slide) & valid for slide in range(slides)]
    for slide in range(slides):
        top = jnp.max(jnp.where(members[slide], scores, -1e30), axis=0, keepdims=True)
        weight = jnp.where(members[slide], jnp.exp(jnp.where(members[slide], scores - top, 0.0)), 0.0)
        total = jnp.sum(weight, axis=0, keepdims=True)
        dots = jnp.sum(weight * class_dot, axis=0, keepdims=True)
        part[slide:slide + 1, :] = jnp.where(first[:1], top, pltpu.roll(total, queries, axis=1))
        part[slides + slide:slides + slide + 1, :] = jnp.where(first[:1], dots, 0.0)

    pl.semaphore_wait(barrier, count - 1)

    def part_copy(hop, slot):
        return pltpu.make_async_remote_copy(
            src_ref=part, dst_ref=parts_all.at[slot], send_sem=part_send.at[hop], recv_sem=part_recv.at[hop],
            device_id={"tile": wrapped(me + hop)}, device_id_type=MESH)

    @pl.loop(1, count)
    def _(hop):
        part_copy(hop, me).start()

    parts_all[me] = part[...]

    @pl.loop(0, out_blocks)
    def _(at):
        cols = pl.ds(pl.multiple_of(at * WIDE, WIDE), WIDE)
        x_turned[cols, :] = x[:, cols].T

    @pl.loop(1, count)
    def _(hop):
        part_copy(hop, wrapped(me - hop + count)).wait_recv()

    gathered = parts_all[...]
    tops = jnp.max(gathered, axis=0)
    rescale = jnp.exp(gathered - tops[None])
    totals = jnp.sum(rescale * pltpu.roll(gathered, queries, axis=2), axis=0)
    ratio = jnp.sum(rescale * pltpu.roll(gathered, slides, axis=1), axis=0) / totals
    used = first & (sub < slides)
    logit = jnp.sum(jnp.where(used, ratio, 0.0), axis=1, keepdims=True) + jnp.zeros((here_tiles, lanes), f32)
    target_vec = jnp.zeros((here_tiles, lanes), jnp.int32)
    for slide in range(slides):
        target_vec = jnp.where(sub == slide, label_ref[slide], target_vec)
    targets = target_vec.astype(f32)
    loss_ref[...] = jnp.maximum(logit, 0.0) + jnp.log1p(jnp.exp(-jnp.abs(logit))) - targets * logit
    dlogit = (jax.nn.sigmoid(logit) - targets) * (1.0 / slides)

    def per_tile(values):
        result = jnp.zeros((here_tiles, lanes), f32)
        for slide in range(slides):
            result = jnp.where(members[slide], values[slide:slide + 1, :], result)
        return result

    live = valid & first
    weights = jnp.where(live, jnp.exp(jnp.where(live, scores - per_tile(tops), 0.0)), 0.0)
    prob_grad = jnp.where(live, weights / jnp.where(live, per_tile(totals), 1.0) * per_tile(dlogit), 0.0)
    dscore = jnp.where(live, prob_grad * (class_dot - per_tile(ratio)), 0.0) * inv_root
    coef = dscore + pltpu.roll(prob_grad, queries, axis=1)
    dembed3 = jnp.dot(jnp.concatenate(three_pieces(coef), axis=0).astype(jnp.bfloat16), both[...],
                      preferred_element_type=f32)
    embed[...] = (dembed3[:here_tiles] + dembed3[here_tiles:2 * here_tiles] + dembed3[2 * here_tiles:]) * (1.0 / positions)

    partners = [me + (1 << bit) * (1 - 2 * ((me // (1 << bit)) % 2)) for bit in range(steps)]

    def span(order, step, unit):
        half = count >> (step + 1)
        base = 0
        for at in range(step):
            base = base + ((me // (1 << order[at])) % 2) * (count >> (at + 1))
        mine = (me // (1 << order[step])) % 2
        keep = pl.multiple_of((base + mine * half) * unit, unit)
        give = pl.multiple_of((base + (1 - mine) * half) * unit, unit)
        return keep, give, half * unit

    def land_at(step, unit):
        return (count - (count >> step)) * unit

    def begin(source, land, order, step, unit, sends, recvs):
        keep, give, size = span(order, step, unit)
        copy = pltpu.make_async_remote_copy(
            src_ref=source.at[pl.ds(give, size)],
            dst_ref=land.at[pl.ds(land_at(step, unit), size)],
            send_sem=sends, recv_sem=recvs,
            device_id={"tile": partners[order[step]]},
            device_id_type=MESH,
        )
        copy.start()
        return copy

    def add(source, land, order, step, unit):
        keep, give, size = span(order, step, unit)
        piece = min(size, 256)

        @pl.loop(0, size // piece)
        def _(at):
            here = pl.ds(pl.multiple_of(keep + at * piece, piece), piece)
            there = pl.ds(pl.multiple_of(land_at(step, unit) + at * piece, piece), piece)
            source[here, :] = source[here, :] + land[there, :]

    copies = {}

    def send(step, chunk):
        copies[step, chunk] = begin(grads[chunk], lands[chunk], orders[chunk], step, unit_rows,
                                    send_sem.at[step, chunk], recv_sem.at[step, chunk])

    query_order = list(range(steps))
    query_copies = []

    def query_start():
        terms = three_pieces(dscore)
        sides = three_pieces(embeds)
        left = jnp.concatenate([terms[0], terms[0], terms[1], terms[1], terms[0], terms[2]], axis=0)
        right = jnp.concatenate([sides[0], sides[1], sides[0], sides[1], sides[2], sides[0]], axis=0)
        product = lax.dot_general(left.astype(jnp.bfloat16), right.astype(jnp.bfloat16), (((0,), (0,)), ((), ())),
                                  preferred_element_type=f32)
        for above in range(queries // 8):
            for beside in range(width // 128):
                at = (above * (width // 128) + beside) * 8
                query_sum[at:at + 8, :] = product[above * 8:above * 8 + 8, beside * 128:beside * 128 + 128]
        query_copies.append(begin(query_sum, query_land, query_order, 0, query_rows,
                                  query_send.at[0], query_recv.at[0]))

    def share(step):
        keep, give, size = span(query_order, step, query_rows)
        held = query_full.at[pl.ds(keep, size)]
        copy = pltpu.make_async_remote_copy(
            src_ref=held, dst_ref=held,
            send_sem=query_send.at[steps + step], recv_sem=query_recv.at[steps + step],
            device_id={"tile": partners[query_order[step]]},
            device_id_type=MESH,
        )
        copy.start()
        return copy

    def advance_query():
        done = len(query_copies) - 1
        query_copies[done].wait()
        if done < steps:
            add(query_sum, query_land, query_order, done, query_rows)
        if done < steps - 1:
            query_copies.append(begin(query_sum, query_land, query_order, done + 1, query_rows,
                                      query_send.at[done + 1], query_recv.at[done + 1]))
            return
        if done == steps - 1:
            own = pl.ds(pl.multiple_of(place_of(me, query_order) * query_rows, query_rows), query_rows)
            query_full[own, :] = query_sum[own, :]
        query_copies.append(share(2 * steps - 2 - done) if done < 2 * steps - 1 else None)

    query_start()
    for at in range(out_blocks):
        cols = slice(at * WIDE, (at + 1) * WIDE)
        block = jnp.concatenate(
            [slope_out[tile * positions:(tile + 1) * positions, cols] * embed[tile:tile + 1, cols]
             for tile in range(here_tiles)], axis=0).astype(jnp.bfloat16)
        dout[:, cols] = block
        dout_turned[cols, :] = block.T

    def multiply(left, right, right_cols, chunk):
        for at in range(width // TALL):
            product = jnp.dot(left[at * TALL:(at + 1) * TALL, :], right[:, right_cols], preferred_element_type=f32)
            for inner in range(TALL // rows):
                for part in range(per_block):
                    side, half = part // SPLIT, part % SPLIT
                    place = place_of(at * (TALL // rows) + inner, orders[chunk + part]) * unit_rows
                    start = inner * rows + half * unit_rows
                    grads[chunk + part][place:place + unit_rows, :] = product[
                        start:start + unit_rows, side * CHUNK:(side + 1) * CHUNK]

    def produce(chunk):
        first_col = chunk % per_matrix // per_block * WIDE
        cols = slice(first_col, first_col + WIDE)
        if chunk < per_matrix:
            multiply(dout_turned, hidden, cols, chunk)
        else:
            dmid = lax.dot_general(dout[...], we[cols, :], (((1,), (1,)), ((), ())), preferred_element_type=f32)
            dpre[...] = (dmid * slope_mid[:, cols]).astype(jnp.bfloat16)
            multiply(x_turned, dpre, slice(0, WIDE), chunk)
        for part in range(per_block):
            send(0, chunk + part)

    last_produce = min(order_of_steps)
    for code in order_of_steps:
        chunk, step = code // 16, code % 16
        if code < 0:
            produce((-1 - code) * per_block)
            if code == last_produce:

                @pl.loop(1, count)
                def _(hop):
                    part_copy(hop, me).wait_send()

            continue
        if chunk == chunks:
            advance_query()
            if len(query_copies) > 2 * steps:
                for above in range(queries // 8):
                    for beside in range(width // 128):
                        at = (above * (width // 128) + beside) * 8
                        query_out_ref[above * 8:above * 8 + 8, beside * 128:beside * 128 + 128] = query_full[at:at + 8, :]
            continue
        order = orders[chunk]
        copies[step - 1, chunk].wait()
        add(grads[chunk], lands[chunk], order, step - 1, unit_rows)
        if step < steps:
            send(step, chunk)
        else:
            out_ref = (exp_ref, red_ref)[chunk // per_matrix]
            start = chunk % per_matrix // SPLIT * CHUNK
            top = chunk % SPLIT * unit_rows
            out_ref[top:top + unit_rows, start:start + CHUNK] = grads[chunk][
                pl.ds(pl.multiple_of(place_of(me, order) * unit_rows, unit_rows), unit_rows), :
            ]


def hand_over_kernel(red_in, exp_in, query_in, loss_in, loss_out, query_out, red_out, exp_out, sems):
    copies = [
        pltpu.make_async_copy(source, target, sems.at[at])
        for at, (source, target) in enumerate(((query_in, query_out), (red_in, red_out), (exp_in, exp_out)))
    ]
    for copy in copies:
        copy.start()
    for slide in range(loss_out.shape[0]):
        loss_out[slide] = loss_in[slide, 0]
    for copy in copies:
        copy.wait()


def on_device(count, tiles, slide_of, valid_count, labels, w_reduce, w_expand, queries, cls_weight):
    here_tiles, positions, width = tiles.shape
    slides = labels.shape[0]
    middle = w_reduce.shape[1]
    count_queries = queries.shape[0]
    rows_here = here_tiles * positions
    orders, order_of_steps = plan_of(count, 2 * middle // WIDE)
    steps = len(orders[0])
    chunks = len(orders)
    lanes = 2 * count_queries
    vmem = pl.BlockSpec(memory_space=pltpu.VMEM)
    smem = pl.BlockSpec(memory_space=pltpu.SMEM)
    anywhere = pl.BlockSpec(memory_space=pl.ANY)
    f32, bf16 = jnp.float32, jnp.bfloat16
    flat = (count_queries * width // 128, 128)
    red, exp, shared, loss = pl.pallas_call(
        functools.partial(step_kernel, count, slides, positions, orders, order_of_steps),
        out_shape=(
            pltpu.VMEM((width // count, middle), f32),
            pltpu.VMEM((width // count, middle), f32),
            pltpu.VMEM((count_queries, width), f32),
            pltpu.VMEM((here_tiles, lanes), f32),
        ),
        in_specs=[anywhere] * 8,
        out_specs=(vmem,) * 4,
        scratch_shapes=(
            [pltpu.VMEM((width // SPLIT, CHUNK), f32)] * (2 * chunks)
            + [
                pltpu.VMEM((rows_here, width), bf16),
                pltpu.VMEM((width, middle), bf16),
                pltpu.VMEM((middle, width), bf16),
                pltpu.VMEM((lanes, width), bf16),
                pltpu.VMEM((rows_here, middle), bf16),
                pltpu.VMEM((rows_here, middle), f32),
                pltpu.VMEM((rows_here, width), f32),
                pltpu.VMEM((rows_here, width), bf16),
                pltpu.VMEM((rows_here, WIDE), bf16),
                pltpu.VMEM((here_tiles, width), f32),
                pltpu.VMEM((here_tiles, lanes), f32),
                pltpu.VMEM((count, here_tiles, lanes), f32),
                pltpu.SMEM(slide_of.shape, jnp.int32),
                pltpu.SMEM(valid_count.shape, jnp.int32),
                pltpu.SMEM(labels.shape, jnp.int32),
                pltpu.VMEM(flat, f32),
                pltpu.VMEM(flat, f32),
                pltpu.VMEM(flat, f32),
                pltpu.SemaphoreType.DMA((7 + middle // WIDE,)),
                pltpu.SemaphoreType.DMA((count,)),
                pltpu.SemaphoreType.DMA((count,)),
                pltpu.SemaphoreType.DMA((steps, chunks)),
                pltpu.SemaphoreType.DMA((steps, chunks)),
                pltpu.SemaphoreType.DMA((2 * steps,)),
                pltpu.SemaphoreType.DMA((2 * steps,)),
            ]
        ),
        compiler_params=pltpu.CompilerParams(
            collective_id=0, has_side_effects=True, vmem_limit_bytes=60 * 1024 * 1024
        ),
    )(slide_of, valid_count, labels, tiles.reshape(rows_here, width), w_reduce, w_expand, queries, cls_weight)
    held = [pltpu.with_memory_space_constraint(value, pltpu.VMEM) for value in (red, exp, shared, loss)]
    return pl.pallas_call(
        hand_over_kernel,
        out_shape=(
            jax.ShapeDtypeStruct((slides,), f32),
            jax.ShapeDtypeStruct(shared.shape, f32),
            jax.ShapeDtypeStruct(red.shape, f32),
            jax.ShapeDtypeStruct(exp.shape, f32),
        ),
        in_specs=[vmem] * 4,
        out_specs=(smem,) + (anywhere,) * 3,
        scratch_shapes=[pltpu.SemaphoreType.DMA((3,))],
    )(*held)


def solution(mesh):
    return jax.shard_map(
        functools.partial(on_device, mesh.shape["tile"]),
        mesh=mesh,
        in_specs=(
            P(("groups", "tile"), None, None),
            P(("groups", "tile")),
            P(("groups", "tile")),
            P("groups"),
            P(),
            P(),
            P(),
            P(),
        ),
        out_specs=(
            P("groups"),
            P("groups", None),
            P(("groups", "tile"), None),
            P(("groups", "tile"), None),
        ),
        check_vma=False,
    )
```

```python
import functools

import jax
import jax.numpy as jnp
import numpy as np
from jax import lax
from jax.experimental import pallas as pl
from jax.experimental.pallas import tpu as pltpu
from jax.sharding import PartitionSpec as P

CHUNK = 128
WIDE = 256
TALL = 512
LAG = 4
SPLIT = 1
KINDS = (
    2, 0, 1, 2, 0, 2, 0, 1, 0, 1, 1, 2, 0, 0, 1, 1,
)
STEPS = (
    -1, 257, -2, 1, -3, 33, 17, 65, 81, 258, -4, -5, -6, 113, 259, 161, 2, 97, 177, -7, 34, -8, 260, 49,
    66, 114, 18, 98, 82, 145, 162, 35, 193, 19, 261, 241, 209, 99, 178, 194, 115, 67, 129, 50, 210, 163, 146, 262,
    68, 195, 225, 130, 242, 116, 83, 100, 3, 211, 20, 164, 196, 243, 147, 226, 263, 212, 36, 69, 4, 179, 51, 131,
    197, 101, 21, 244, 227, 264, 213, 84, 180, 148, 132, 37, 52, 117, 228, 265, 165, 181, 5, 245, 266, 53, 149, 85,
    133, 229,
)
MESH = pl.DeviceIdType.MESH


def plan_of(count, blocks):
    bits = count.bit_length() - 1
    parts = blocks * (WIDE // CHUNK) * SPLIT
    if (bits, blocks) == (5, 8):
        orders = [[0, 1, 2, 3, 4], [0, 2, 1, 3, 4], [0, 3, 4, 1, 2]]
        return [orders[kind] for kind in KINDS], STEPS
    ring = list(range(1, bits))
    turns = [ring[turn:] + ring[:turn] for turn in (0, 1, 2)]
    orders = [[0] + turns[part // SPLIT % 8 % 3] for part in range(parts)]
    per_block = parts // blocks
    keyed = []
    for part in range(parts):
        if part % per_block == 0:
            keyed.append((part / SPLIT, -1 - part // per_block))
        for step in range(1, bits + 1):
            keyed.append((part / SPLIT + LAG * step, part * 16 + step))
    for step in range(1, 2 * bits + 1):
        keyed.append((step * 0.5 * LAG, parts * 16 + step))
    return orders, [code for key, code in sorted(keyed, key=lambda pair: pair[0])]


def place_of(block, order):
    place = 0
    for bit in order:
        place = place * 2 + (block // (1 << bit)) % 2
    return place


def three_pieces(values):
    high = values.astype(jnp.bfloat16).astype(jnp.float32)
    rest = values - high
    middle = rest.astype(jnp.bfloat16).astype(jnp.float32)
    return high, middle, rest - middle


def step_kernel(count, slides, positions, orders, order_of_steps, slide_any, valid_any, label_any, tiles_ref, reduce_ref, expand_ref,
                query_ref, class_ref, red_ref, exp_ref, query_out_ref, loss_ref, *scratch):
    width, middle = reduce_ref.shape
    rows_here = tiles_ref.shape[0]
    here_tiles = rows_here // positions
    queries = query_ref.shape[0]
    lanes = 2 * queries
    per_matrix = middle // CHUNK * SPLIT
    per_block = WIDE // CHUNK * SPLIT
    chunks = 2 * per_matrix
    grads = scratch[:chunks]
    lands = scratch[chunks:2 * chunks]
    (x, wr, we, both, hidden, slope_mid, slope_out, dout, dpre, embed, part, parts_all, slide_ref, valid_ref, label_ref,
     query_sum, query_land, query_full, load_sem, part_send, part_recv, send_sem, recv_sem, query_send, query_recv,
     ) = scratch[2 * chunks:]
    steps = len(orders[0])
    me = lax.axis_index("tile")
    turned = [wr.at[:, pl.ds(side * rows_here, rows_here)] for side in (0, 1)]
    x_turned, dout_turned = turned
    rows = width // count
    unit_rows = rows // SPLIT
    query_rows = query_sum.shape[0] // count
    inv_root = np.float32(1.0) / np.sqrt(np.float32(width))
    f32 = jnp.float32

    barrier = pltpu.get_barrier_semaphore()

    mid_blocks = middle // WIDE
    out_blocks = width // WIDE
    def load(source, target, at):
        copy = pltpu.make_async_copy(source, target, load_sem.at[at])
        copy.start()
        return copy
    def columns(ref, at):
        return ref.at[:, pl.ds(at * WIDE, WIDE)]
    x_load = load(tiles_ref, x, 0)
    for at in range(mid_blocks):
        load(columns(reduce_ref, at), columns(wr, at), 4 + at)
    we_load = load(expand_ref, we, 1)
    both_loads = [load(query_ref, both.at[pl.ds(0, queries)], 2), load(class_ref, both.at[pl.ds(queries, queries)], 3)]

    small_loads = [load(slide_any, slide_ref, 4 + mid_blocks), load(valid_any, valid_ref, 5 + mid_blocks),
                   load(label_any, label_ref, 6 + mid_blocks)]

    def wrapped(device):
        return jnp.where(device >= count, device - count, device)

    @pl.loop(1, count)
    def _(hop):
        pl.semaphore_signal(barrier, inc=1, device_id={"tile": wrapped(me + hop)}, device_id_type=MESH)

    x_load.wait()

    @pl.loop(0, mid_blocks)
    def _(at):
        cols = pl.ds(pl.multiple_of(at * WIDE, WIDE), WIDE)
        pltpu.make_async_copy(reduce_ref.at[:, cols], wr.at[:, cols], load_sem.at[4 + at]).wait()
        pre = jnp.dot(x[...], wr[:, cols], preferred_element_type=f32)
        sig = 0.5 * jnp.tanh(0.5 * pre) + 0.5
        act = pre * sig
        hidden[:, cols] = act.astype(jnp.bfloat16)
        slope_mid[:, cols] = sig + act * (1.0 - sig)
    we_load.wait()

    @pl.loop(0, width // (2 * TALL))
    def _(at):
        cols = pl.ds(pl.multiple_of(at * 2 * TALL, 2 * TALL), 2 * TALL)
        pre = x[:, cols].astype(f32) + jnp.dot(hidden[...], we[:, cols], preferred_element_type=f32)
        sig = 0.5 * jnp.tanh(0.5 * pre) + 0.5
        act = pre * sig
        slope_out[:, cols] = sig + act * (1.0 - sig)
        embed[:, cols] = jnp.sum(act.reshape(here_tiles, positions, 2 * TALL), axis=1) * (1.0 / positions)

    for copy in both_loads + small_loads:
        copy.wait()

    embeds = embed[...]
    pieces = three_pieces(embeds)
    score3 = lax.dot_general(jnp.concatenate(pieces, axis=0).astype(jnp.bfloat16), both[...],
                             (((1,), (1,)), ((), ())), preferred_element_type=f32)
    both_dot = score3[:here_tiles] + score3[here_tiles:2 * here_tiles] + score3[2 * here_tiles:]
    sub = lax.broadcasted_iota(jnp.int32, (here_tiles, lanes), 0)
    lane = lax.broadcasted_iota(jnp.int32, (here_tiles, lanes), 1)
    first = lane < queries
    scores = both_dot * inv_root
    class_dot = pltpu.roll(both_dot, queries, axis=1)
    slide_vec = jnp.zeros((here_tiles, lanes), jnp.int32)
    for tile in range(here_tiles):
        slide_vec = jnp.where(sub == tile, slide_ref[tile], slide_vec)
    valid = sub < valid_ref[0]
    members = [(slide_vec == slide) & valid for slide in range(slides)]
    for slide in range(slides):
        top = jnp.max(jnp.where(members[slide], scores, -1e30), axis=0, keepdims=True)
        weight = jnp.where(members[slide], jnp.exp(jnp.where(members[slide], scores - top, 0.0)), 0.0)
        total = jnp.sum(weight, axis=0, keepdims=True)
        dots = jnp.sum(weight * class_dot, axis=0, keepdims=True)
        part[slide:slide + 1, :] = jnp.where(first[:1], top, pltpu.roll(total, queries, axis=1))
        part[slides + slide:slides + slide + 1, :] = jnp.where(first[:1], dots, 0.0)

    pl.semaphore_wait(barrier, count - 1)

    def part_copy(hop, slot):
        return pltpu.make_async_remote_copy(
            src_ref=part, dst_ref=parts_all.at[slot], send_sem=part_send.at[hop], recv_sem=part_recv.at[hop],
            device_id={"tile": wrapped(me + hop)}, device_id_type=MESH)

    @pl.loop(1, count)
    def _(hop):
        part_copy(hop, me).start()

    parts_all[me] = part[...]

    @pl.loop(0, out_blocks)
    def _(at):
        cols = pl.ds(pl.multiple_of(at * WIDE, WIDE), WIDE)
        x_turned[cols, :] = x[:, cols].T

    @pl.loop(1, count)
    def _(hop):
        part_copy(hop, wrapped(me - hop + count)).wait_recv()

    gathered = parts_all[...]
    tops = jnp.max(gathered, axis=0)
    rescale = jnp.exp(gathered - tops[None])
    totals = jnp.sum(rescale * pltpu.roll(gathered, queries, axis=2), axis=0)
    ratio = jnp.sum(rescale * pltpu.roll(gathered, slides, axis=1), axis=0) / totals
    used = first & (sub < slides)
    logit = jnp.sum(jnp.where(used, ratio, 0.0), axis=1, keepdims=True) + jnp.zeros((here_tiles, lanes), f32)
    target_vec = jnp.zeros((here_tiles, lanes), jnp.int32)
    for slide in range(slides):
        target_vec = jnp.where(sub == slide, label_ref[slide], target_vec)
    targets = target_vec.astype(f32)
    loss_ref[...] = jnp.maximum(logit, 0.0) + jnp.log1p(jnp.exp(-jnp.abs(logit))) - targets * logit
    dlogit = (jax.nn.sigmoid(logit) - targets) * (1.0 / slides)

    def per_tile(values):
        result = jnp.zeros((here_tiles, lanes), f32)
        for slide in range(slides):
            result = jnp.where(members[slide], values[slide:slide + 1, :], result)
        return result

    live = valid & first
    weights = jnp.where(live, jnp.exp(jnp.where(live, scores - per_tile(tops), 0.0)), 0.0)
    prob_grad = jnp.where(live, weights / jnp.where(live, per_tile(totals), 1.0) * per_tile(dlogit), 0.0)
    dscore = jnp.where(live, prob_grad * (class_dot - per_tile(ratio)), 0.0) * inv_root
    coef = dscore + pltpu.roll(prob_grad, queries, axis=1)
    dembed3 = jnp.dot(jnp.concatenate(three_pieces(coef), axis=0).astype(jnp.bfloat16), both[...],
                      preferred_element_type=f32)
    embed[...] = (dembed3[:here_tiles] + dembed3[here_tiles:2 * here_tiles] + dembed3[2 * here_tiles:]) * (1.0 / positions)

    partners = [me + (1 << bit) * (1 - 2 * ((me // (1 << bit)) % 2)) for bit in range(steps)]

    def span(order, step, unit):
        half = count >> (step + 1)
        base = 0
        for at in range(step):
            base = base + ((me // (1 << order[at])) % 2) * (count >> (at + 1))
        mine = (me // (1 << order[step])) % 2
        keep = pl.multiple_of((base + mine * half) * unit, unit)
        give = pl.multiple_of((base + (1 - mine) * half) * unit, unit)
        return keep, give, half * unit

    def land_at(step, unit):
        return (count - (count >> step)) * unit

    def begin(source, land, order, step, unit, sends, recvs):
        keep, give, size = span(order, step, unit)
        copy = pltpu.make_async_remote_copy(
            src_ref=source.at[pl.ds(give, size)],
            dst_ref=land.at[pl.ds(land_at(step, unit), size)],
            send_sem=sends, recv_sem=recvs,
            device_id={"tile": partners[order[step]]},
            device_id_type=MESH,
        )
        copy.start()
        return copy

    def add(source, land, order, step, unit):
        keep, give, size = span(order, step, unit)
        piece = min(size, 256)

        @pl.loop(0, size // piece)
        def _(at):
            here = pl.ds(pl.multiple_of(keep + at * piece, piece), piece)
            there = pl.ds(pl.multiple_of(land_at(step, unit) + at * piece, piece), piece)
            source[here, :] = source[here, :] + land[there, :]

    copies = {}

    def send(step, chunk):
        copies[step, chunk] = begin(grads[chunk], lands[chunk], orders[chunk], step, unit_rows,
                                    send_sem.at[step, chunk], recv_sem.at[step, chunk])

    query_order = list(range(steps))
    query_copies = []

    def query_start():
        terms = three_pieces(dscore)
        sides = three_pieces(embeds)
        left = jnp.concatenate([terms[0], terms[0], terms[1], terms[1], terms[0], terms[2]], axis=0)
        right = jnp.concatenate([sides[0], sides[1], sides[0], sides[1], sides[2], sides[0]], axis=0)
        product = lax.dot_general(left.astype(jnp.bfloat16), right.astype(jnp.bfloat16), (((0,), (0,)), ((), ())),
                                  preferred_element_type=f32)
        for above in range(queries // 8):
            for beside in range(width // 128):
                at = (above * (width // 128) + beside) * 8
                query_sum[at:at + 8, :] = product[above * 8:above * 8 + 8, beside * 128:beside * 128 + 128]
        query_copies.append(begin(query_sum, query_land, query_order, 0, query_rows,
                                  query_send.at[0], query_recv.at[0]))

    def share(step):
        keep, give, size = span(query_order, step, query_rows)
        held = query_full.at[pl.ds(keep, size)]
        copy = pltpu.make_async_remote_copy(
            src_ref=held, dst_ref=held,
            send_sem=query_send.at[steps + step], recv_sem=query_recv.at[steps + step],
            device_id={"tile": partners[query_order[step]]},
            device_id_type=MESH,
        )
        copy.start()
        return copy

    def advance_query():
        done = len(query_copies) - 1
        query_copies[done].wait()
        if done < steps:
            add(query_sum, query_land, query_order, done, query_rows)
        if done < steps - 1:
            query_copies.append(begin(query_sum, query_land, query_order, done + 1, query_rows,
                                      query_send.at[done + 1], query_recv.at[done + 1]))
            return
        if done == steps - 1:
            own = pl.ds(pl.multiple_of(place_of(me, query_order) * query_rows, query_rows), query_rows)
            query_full[own, :] = query_sum[own, :]
        query_copies.append(share(2 * steps - 2 - done) if done < 2 * steps - 1 else None)

    query_start()
    for at in range(out_blocks):
        cols = slice(at * WIDE, (at + 1) * WIDE)
        block = jnp.concatenate(
            [slope_out[tile * positions:(tile + 1) * positions, cols] * embed[tile:tile + 1, cols]
             for tile in range(here_tiles)], axis=0).astype(jnp.bfloat16)
        dout[:, cols] = block
        dout_turned[cols, :] = block.T

    def multiply(left, right, right_cols, chunk):
        for at in range(width // TALL):
            product = jnp.dot(left[at * TALL:(at + 1) * TALL, :], right[:, right_cols], preferred_element_type=f32)
            for inner in range(TALL // rows):
                for part in range(per_block):
                    side, half = part // SPLIT, part % SPLIT
                    place = place_of(at * (TALL // rows) + inner, orders[chunk + part]) * unit_rows
                    start = inner * rows + half * unit_rows
                    grads[chunk + part][place:place + unit_rows, :] = product[
                        start:start + unit_rows, side * CHUNK:(side + 1) * CHUNK]

    def produce(chunk):
        first_col = chunk % per_matrix // per_block * WIDE
        cols = slice(first_col, first_col + WIDE)
        if chunk < per_matrix:
            multiply(dout_turned, hidden, cols, chunk)
        else:
            dmid = lax.dot_general(dout[...], we[cols, :], (((1,), (1,)), ((), ())), preferred_element_type=f32)
            dpre[...] = (dmid * slope_mid[:, cols]).astype(jnp.bfloat16)
            multiply(x_turned, dpre, slice(0, WIDE), chunk)
        for part in range(per_block):
            send(0, chunk + part)

    last_produce = min(order_of_steps)
    for code in order_of_steps:
        chunk, step = code // 16, code % 16
        if code < 0:
            produce((-1 - code) * per_block)
            if code == last_produce:

                @pl.loop(1, count)
                def _(hop):
                    part_copy(hop, me).wait_send()

            continue
        if chunk == chunks:
            advance_query()
            if len(query_copies) > 2 * steps:
                for above in range(queries // 8):
                    for beside in range(width // 128):
                        at = (above * (width // 128) + beside) * 8
                        query_out_ref[above * 8:above * 8 + 8, beside * 128:beside * 128 + 128] = query_full[at:at + 8, :]
            continue
        order = orders[chunk]
        copies[step - 1, chunk].wait()
        add(grads[chunk], lands[chunk], order, step - 1, unit_rows)
        if step < steps:
            send(step, chunk)
        else:
            out_ref = (exp_ref, red_ref)[chunk // per_matrix]
            start = chunk % per_matrix // SPLIT * CHUNK
            top = chunk % SPLIT * unit_rows
            out_ref[top:top + unit_rows, start:start + CHUNK] = grads[chunk][
                pl.ds(pl.multiple_of(place_of(me, order) * unit_rows, unit_rows), unit_rows), :
            ]


def hand_over_kernel(red_in, exp_in, query_in, loss_in, loss_out, query_out, red_out, exp_out, sems):
    copies = [
        pltpu.make_async_copy(source, target, sems.at[at])
        for at, (source, target) in enumerate(((query_in, query_out), (red_in, red_out), (exp_in, exp_out)))
    ]
    for copy in copies:
        copy.start()
    for slide in range(loss_out.shape[0]):
        loss_out[slide] = loss_in[slide, 0]
    for copy in copies:
        copy.wait()


def on_device(count, tiles, slide_of, valid_count, labels, w_reduce, w_expand, queries, cls_weight):
    here_tiles, positions, width = tiles.shape
    slides = labels.shape[0]
    middle = w_reduce.shape[1]
    count_queries = queries.shape[0]
    rows_here = here_tiles * positions
    orders, order_of_steps = plan_of(count, 2 * middle // WIDE)
    steps = len(orders[0])
    chunks = len(orders)
    lanes = 2 * count_queries
    vmem = pl.BlockSpec(memory_space=pltpu.VMEM)
    smem = pl.BlockSpec(memory_space=pltpu.SMEM)
    anywhere = pl.BlockSpec(memory_space=pl.ANY)
    in_hbm = pl.BlockSpec(memory_space=pltpu.HBM)
    f32, bf16 = jnp.float32, jnp.bfloat16
    flat = (count_queries * width // 128, 128)
    red, exp, shared, loss = pl.pallas_call(
        functools.partial(step_kernel, count, slides, positions, orders, order_of_steps),
        out_shape=(
            pltpu.VMEM((width // count, middle), f32),
            pltpu.VMEM((width // count, middle), f32),
            pltpu.VMEM((count_queries, width), f32),
            pltpu.VMEM((here_tiles, lanes), f32),
        ),
        in_specs=[in_hbm] * 8,
        out_specs=(vmem,) * 4,
        scratch_shapes=(
            [pltpu.VMEM((width // SPLIT, CHUNK), f32)] * (2 * chunks)
            + [
                pltpu.VMEM((rows_here, width), bf16),
                pltpu.VMEM((width, middle), bf16),
                pltpu.VMEM((middle, width), bf16),
                pltpu.VMEM((lanes, width), bf16),
                pltpu.VMEM((rows_here, middle), bf16),
                pltpu.VMEM((rows_here, middle), f32),
                pltpu.VMEM((rows_here, width), f32),
                pltpu.VMEM((rows_here, width), bf16),
                pltpu.VMEM((rows_here, WIDE), bf16),
                pltpu.VMEM((here_tiles, width), f32),
                pltpu.VMEM((here_tiles, lanes), f32),
                pltpu.VMEM((count, here_tiles, lanes), f32),
                pltpu.SMEM(slide_of.shape, jnp.int32),
                pltpu.SMEM(valid_count.shape, jnp.int32),
                pltpu.SMEM(labels.shape, jnp.int32),
                pltpu.VMEM(flat, f32),
                pltpu.VMEM(flat, f32),
                pltpu.VMEM(flat, f32),
                pltpu.SemaphoreType.DMA((7 + middle // WIDE,)),
                pltpu.SemaphoreType.DMA((count,)),
                pltpu.SemaphoreType.DMA((count,)),
                pltpu.SemaphoreType.DMA((steps, chunks)),
                pltpu.SemaphoreType.DMA((steps, chunks)),
                pltpu.SemaphoreType.DMA((2 * steps,)),
                pltpu.SemaphoreType.DMA((2 * steps,)),
            ]
        ),
        compiler_params=pltpu.CompilerParams(
            collective_id=0, has_side_effects=True, vmem_limit_bytes=60 * 1024 * 1024
        ),
    )(slide_of, valid_count, labels, tiles.reshape(rows_here, width), w_reduce, w_expand, queries, cls_weight)
    held = [pltpu.with_memory_space_constraint(value, pltpu.VMEM) for value in (red, exp, shared, loss)]
    return pl.pallas_call(
        hand_over_kernel,
        out_shape=(
            jax.ShapeDtypeStruct((slides,), f32),
            jax.ShapeDtypeStruct(shared.shape, f32),
            jax.ShapeDtypeStruct(red.shape, f32),
            jax.ShapeDtypeStruct(exp.shape, f32),
        ),
        in_specs=[vmem] * 4,
        out_specs=(smem,) + (anywhere,) * 3,
        scratch_shapes=[pltpu.SemaphoreType.DMA((3,))],
    )(*held)


def solution(mesh):
    return jax.shard_map(
        functools.partial(on_device, mesh.shape["tile"]),
        mesh=mesh,
        in_specs=(
            P(("groups", "tile"), None, None),
            P(("groups", "tile")),
            P(("groups", "tile")),
            P("groups"),
            P(),
            P(),
            P(),
            P(),
        ),
        out_specs=(
            P("groups"),
            P("groups", None),
            P(("groups", "tile"), None),
            P(("groups", "tile"), None),
        ),
        check_vma=False,
    )
```
